512 devices in a mesh: dom: 512 (over y, z, x, core).
Axes of the slice: x: 4, y: 4, z: 16, core: 2. Of those that a mesh axis runs over, the one named last changes fastest.
Arguments:
- dof_values: float32 [9, 20, 131072], P(None, None, 'dom'), may hold values from -6 to 6
- star_mats: bfloat16 [3, 9, 9, 131072], P(None, None, None, 'dom'), may hold values from -0.1796875 to 0.1796875
- flux_local: bfloat16 [4, 9, 9, 131072], P(None, None, None, 'dom'), may hold values from -0.19921875 to 0.19921875
- flux_neigh: bfloat16 [4, 9, 9, 131072], P(None, None, None, 'dom'), may hold values from -0.19921875 to 0.19921875
- kstiff: float32 [3, 20, 20], replicated, may hold values from -1.25 to 1.25
- flux_minus: float32 [4, 20, 20], replicated, may hold values from -1.25 to 1.25
- flux_plus: float32 [4, 4, 20, 20], replicated, may hold values from -1.25 to 1.25
- neighbour: int32 [4, 131072], P(None, 'dom'), may hold values from 0 to 511, as said below
- neigh_face: int32 [4, 131072], P(None, 'dom'), may hold values from 0 to 3
- cluster: int32 [131072], P('dom'), may hold values from 0 to 1
- send_list: int32 [512, 4, 64], P('dom'), may hold values from 0 to 255
- damage_list: int32 [512, 256], P('dom'), may hold values from 0 to 255, as said below
- damage_count: int32 [512], P('dom'), may hold values from 0 to 256, as said below
- yield_mask: int32 [20, 131072], P(None, 'dom'), may hold values 0 or 1
- cohesion: float32 [131072], P('dom'), may hold values from 0.3 to 3
- to_points: float32 [20, 20], replicated, may hold values from -1.25 to 1.25
- from_points: float32 [20, 20], replicated, may hold values from -1.25 to 1.25
Outputs:
- new_dofs: float32 [9, 20, 131072], P(None, None, 'dom')
The draws below stay inside these ranges and needn't reach their ends.
Inputs may be any that keep to these rules, and one draw needn't show every extreme that they name: `neighbour`: entries below 256 are elements of the same partition; the entry 256 + j * 64 + i names ghost slot i of offset slot j. `damage_list`: the entries of one partition's row are distinct. `damage_count`: some partition has exactly 256.
All inputs are finite; a program needn't handle non-finite values. No bound on the sum of `yield_mask` on one device may be relied on, other than what follows from the above.
Results may differ from the reference program's by a relative error of at most 0.0003.
Values sent between devices are 32-bit elements; how exact they have to be, the bound alone decides.
A program may use at most 128 MiB of HBM per device.

```python
import math
import jax
import jax.numpy as jnp
from jax import lax

NQTY = 9
NBASIS = 20
NQP = 20
NDER = 3
NOFF = 4
E_DEV = 256
NB = 64
NDMG = 256
ELEMS = 131072
N_DOM = 512


def draw_neighbour(key, part):
    choose_key, local_key, ghost_key = jax.random.split(key, 3)
    choose_kind = jax.random.randint(choose_key, (4, ELEMS), 0, 5)
    local_ids = jax.random.randint(local_key, (4, ELEMS), 0, E_DEV)
    ghost_ids = jax.random.randint(ghost_key, (4, ELEMS), E_DEV, E_DEV + NOFF * NB)
    return jnp.where(choose_kind == 0, ghost_ids, local_ids).astype(jnp.int32)


def draw_damage_list(key, part):
    row_keys = jax.random.split(key, N_DOM)

    def one_row(row_key):
        return jax.random.permutation(row_key, E_DEV)[:NDMG]
    return jax.vmap(one_row)(row_keys).astype(jnp.int32)


def draw_damage_count(key, part):
    count_key, top_key = jax.random.split(key)
    counts = jax.random.randint(count_key, (N_DOM,), NDMG // 16, NDMG + 1)
    busiest = jax.random.randint(top_key, (), 0, N_DOM)
    return counts.at[busiest].set(NDMG).astype(jnp.int32)


def plant(drawn, key, smallest, top_value):
    place = [jax.random.randint(jax.random.fold_in(key, axis), (), 0, length) for axis, length in enumerate(drawn.shape)]
    widest = drawn.shape.index(max(drawn.shape))
    beside = place[:widest] + [(place[widest] + 1) % drawn.shape[widest]] + place[widest + 1:]
    return drawn.at[tuple(place)].set(smallest).at[tuple(beside)].set(top_value)


def block_scale(rng, extent, cuts, low, largest):
    loudness, own = 1.0, jax.random.fold_in(rng, 6)
    for position, parts in cuts:
        draws = jnp.exp(jax.random.uniform(jax.random.fold_in(own, position), (parts,), jnp.float32, low / len(cuts), largest / len(cuts)))
        loudness = loudness * jnp.repeat(draws, extent[position] // parts).reshape([-1 if axis == position else 1 for axis in range(len(extent))])
    return loudness


def noise(key, extent, spread, bound, cuts=(), held_as=jnp.bfloat16):
    drawn = jax.random.normal(key, extent, jnp.float32) * spread
    if len(cuts) > 0:
        drawn = block_scale(key, extent, cuts, -0.22, 0.18) * drawn
    return jnp.clip(drawn, min=-bound, max=bound).astype(held_as)


def setup_inputs(seed: int = 0) -> dict:
    key_list = jax.random.split(jax.random.key(seed), 18)
    dof_values = noise(key_list[0], (NQTY, NBASIS, ELEMS), 1.0, 6.0, ((2, 512),), jnp.float32)
    star_mats = noise(key_list[1], (3, NQTY, NQTY, ELEMS), 0.03, 0.1796875, ((3, 512),))
    flux_local = noise(key_list[2], (4, NQTY, NQTY, ELEMS), 0.035, 0.19921875, ((3, 512),))
    flux_neigh = noise(key_list[3], (4, NQTY, NQTY, ELEMS), 0.035, 0.19921875, ((3, 512),))
    kstiff = noise(key_list[4], (3, NBASIS, NBASIS), NBASIS ** -0.5, 1.25, (), jnp.float32)
    flux_minus = noise(key_list[5], (4, NBASIS, NBASIS), NBASIS ** -0.5, 1.25, (), jnp.float32)
    flux_plus = noise(key_list[6], (4, 4, NBASIS, NBASIS), NBASIS ** -0.5, 1.25, (), jnp.float32)
    neighbour = draw_neighbour(jax.random.fold_in(key_list[17], 71), 0)
    neigh_face = plant(jax.random.randint(key_list[8], (4, ELEMS), 0, 4), jax.random.fold_in(key_list[8], 1), 0, 3).astype(jnp.int32)
    cluster = plant(jax.random.randint(key_list[9], (ELEMS,), 0, 2), jax.random.fold_in(key_list[9], 1), 0, 1).astype(jnp.int32)
    send_list = plant(jax.random.randint(key_list[10], (N_DOM, NOFF, NB), 0, E_DEV), jax.random.fold_in(key_list[10], 1), 0, E_DEV - 1).astype(jnp.int32)
    damage_list = draw_damage_list(jax.random.fold_in(key_list[17], 71), 0)
    damage_count = draw_damage_count(jax.random.fold_in(key_list[17], 71), 0)
    yield_mask = plant((jax.random.randint(key_list[13], (NQP, ELEMS), 0, 2) < 1).astype(jnp.int32), jax.random.fold_in(key_list[13], 1), 0, 1)
    cohesion = jnp.clip(jnp.exp(math.log(3.0) - 2.3025851 * jax.random.uniform(key_list[14], (ELEMS,), jnp.float32) ** block_scale(key_list[14], (ELEMS,), ((0, 512),), -0.2, 0.2)), 0.3, 3.0)
    to_points = noise(key_list[15], (NQP, NBASIS), NBASIS ** -0.5, 1.25, (), jnp.float32)
    from_points = noise(key_list[16], (NBASIS, NQP), NQP ** -0.5, 1.25, (), jnp.float32)
    return {"dof_values": dof_values, "star_mats": star_mats, "flux_local": flux_local, "flux_neigh": flux_neigh, "kstiff": kstiff, "flux_minus": flux_minus, "flux_plus": flux_plus, "neighbour": neighbour, "neigh_face": neigh_face, "cluster": cluster, "send_list": send_list, "damage_list": damage_list, "damage_count": damage_count, "yield_mask": yield_mask, "cohesion": cohesion, "to_points": to_points, "from_points": from_points}


PRECISE = lax.Precision.HIGHEST
OFFSETS = (1, -1, 2, -2)
FRICTION = 0.6
RELAXATION = 0.5

def star_apply(source, matrix):
    wide = matrix.astype(jnp.float32)
    total = source[0][None, :, :] * wide[0][:, None, :]
    for quantity in range(1, source.shape[0]):
        total = total + source[quantity][None, :, :] * wide[quantity][:, None, :]
    return total

def derivatives(source, star_part, kstiff):
    series = [source]
    for degree in range(NDER - 1):
        latest = series[-1]
        following = jnp.zeros_like(latest)
        for direction in range(3):
            rotated = star_apply(latest, star_part[direction])
            following = following + jnp.einsum('bc,pce->pbe', kstiff[direction], rotated, precision=PRECISE)
        series.append(following)
    return series

def taylor(series, time_begin, time_end):
    summed = jnp.zeros_like(series[0])
    divisor = 1.0
    for degree in range(len(series)):
        divisor = divisor * (degree + 1)
        weight_now = (time_end ** (degree + 1) - time_begin ** (degree + 1)) / divisor
        summed = summed + weight_now * series[degree]
    return summed

def volume(integral, star_part, kstiff):
    summed = jnp.zeros_like(integral)
    for direction in range(3):
        rotated = star_apply(integral, star_part[direction])
        summed = summed + jnp.einsum('cb,pce->pbe', kstiff[direction], rotated, precision=PRECISE)
    return summed

def face_values(extended, neighbours):
    return jnp.stack([jnp.take(extended, neighbours[face_id], axis=2) for face_id in range(4)])

def surface(integral, others, neigh_faces, local_flux, neigh_flux, flux_minus, flux_plus):
    summed = jnp.zeros_like(integral)
    for face_id in range(4):
        own_side = star_apply(integral, local_flux[face_id])
        summed = summed + jnp.einsum('bc,pce->pbe', flux_minus[face_id], own_side, precision=PRECISE)
        far_side = star_apply(others[face_id], neigh_flux[face_id])
        selector = (neigh_faces[face_id][None, :] == jnp.arange(4, dtype=jnp.int32)[:, None]).astype(jnp.float32)
        masked = far_side[None] * selector[:, None, None, :]
        summed = summed + jnp.einsum('hbc,hpce->pbe', flux_plus[face_id], masked, precision=PRECISE)
    return summed

def plastic(stress, strength, plastic_mask, to_points, from_points):
    points = jnp.einsum('nb,qbp->qnp', to_points, stress, precision=PRECISE)
    pressure = (points[0] + points[1] + points[2]) / 3.0
    normal = points[:3] - pressure[None]
    shear_part = points[3:]
    tau_eff = jnp.sqrt(0.5 * lax.optimization_barrier(jnp.sum(normal * normal, axis=0)) + lax.optimization_barrier(jnp.sum(shear_part * shear_part, axis=0)))
    yield_limit = jnp.maximum(strength[None, :] - FRICTION * pressure, 0.5 * strength[None, :])
    rate_now = jnp.where(plastic_mask > 0.5, RELAXATION * (yield_limit / jnp.maximum(tau_eff, yield_limit) - 1.0), 0.0)
    change = jnp.concatenate([normal, shear_part], axis=0) * rate_now[None]
    return jnp.einsum('bn,qnp->qbp', from_points, change, precision=PRECISE)

def to_parts(array):
    shaped = array.reshape(array.shape[:-1] + (N_DOM, E_DEV))
    return jnp.moveaxis(shaped, -2, 0)

def from_parts(array):
    moved = jnp.moveaxis(array, 0, -2)
    return moved.reshape(moved.shape[:-2] + (N_DOM * E_DEV,))

def ghosts(buffers, send_list):

    def pick_rows(buffer, listing):
        return jnp.take(buffer, listing.reshape(-1), axis=2)
    blocks = jax.vmap(pick_rows)(buffers, send_list)
    blocks = blocks.reshape(blocks.shape[:3] + (len(OFFSETS), NB))
    pieces = []
    for slot_id in range(len(OFFSETS)):
        offset = OFFSETS[slot_id]
        one_block = blocks[:, :, :, slot_id, :]
        padding = jnp.zeros((abs(offset),) + one_block.shape[1:], jnp.float32)
        if offset > 0:
            shifted = jnp.concatenate([padding, one_block[:-offset]], axis=0)
        else:
            shifted = jnp.concatenate([one_block[-offset:], padding], axis=0)
        pieces.append(shifted)
    return jnp.concatenate(pieces, axis=3)

def reference(dof_values, star_mats, flux_local, flux_neigh, kstiff, flux_minus, flux_plus, neighbour, neigh_face, cluster, send_list, damage_list, damage_count, yield_mask, cohesion, to_points, from_points):
    parts_dofs = to_parts(dof_values)
    parts_star = to_parts(star_mats)
    parts_local = to_parts(flux_local)
    parts_neigh = to_parts(flux_neigh)
    parts_ids = to_parts(neighbour)
    parts_face = to_parts(neigh_face)
    parts_cluster = to_parts(cluster)
    parts_mask = to_parts(yield_mask)
    parts_strength = to_parts(cohesion)

    def section_one(inputs):
        source, star_part = inputs
        return taylor(derivatives(source, star_part, kstiff), 0.0, 1.0)
    buffer_one = lax.map(section_one, (parts_dofs, parts_star))
    ghost_one = ghosts(buffer_one, send_list)

    def section_two(inputs):
        source, star_part, local_flux, neigh_flux, neighbours, neigh_faces, clusters, own_buffer, own_ghost = inputs
        is_fine = (clusters == 0)[None, None, :]
        others = face_values(jnp.concatenate([own_buffer, own_ghost], axis=2), neighbours)
        updated = source + volume(own_buffer, star_part, kstiff) - surface(own_buffer, others, neigh_faces, local_flux, neigh_flux, flux_minus, flux_plus)
        state_one = jnp.where(is_fine, updated, source)
        series = derivatives(state_one, star_part, kstiff)
        buffer_two = jnp.where(is_fine, taylor(series, 0.0, 1.0), taylor(series, 1.0, 2.0))
        return (state_one, buffer_two)
    state_one, buffer_two = lax.map(section_two, (parts_dofs, parts_star, parts_local, parts_neigh, parts_ids, parts_face, parts_cluster, buffer_one, ghost_one))
    ghost_two = ghosts(buffer_two, send_list)

    def section_three(inputs):
        state_now, star_part, local_flux, neigh_flux, neighbours, neigh_faces, clusters, own_one, own_two, ghost_first, ghost_second, listing, live_count, masks, strength = inputs
        is_fine = (clusters == 0)[None, None, :]
        summed_buffer = own_one + own_two
        fine_side = face_values(jnp.concatenate([own_two, ghost_second], axis=2), neighbours)
        coarse_side = face_values(jnp.concatenate([summed_buffer, ghost_first + ghost_second], axis=2), neighbours)
        others = jnp.where(is_fine[None], fine_side, coarse_side)
        integral = jnp.where(is_fine, own_two, summed_buffer)
        state_two = state_now + volume(integral, star_part, kstiff) - surface(integral, others, neigh_faces, local_flux, neigh_flux, flux_minus, flux_plus)
        stress = jnp.take(state_two[:6], listing, axis=2)
        correction = plastic(stress, jnp.take(strength, listing), jnp.take(masks, listing, axis=1).astype(jnp.float32), to_points, from_points)
        live_slots = (jnp.arange(NDMG, dtype=jnp.int32) < live_count).astype(jnp.float32)
        return state_two.at[:6, :, listing].add(correction * live_slots[None, None, :])
    result = lax.map(section_three, (state_one, parts_star, parts_local, parts_neigh, parts_ids, parts_face, parts_cluster, buffer_one, buffer_two, ghost_one, ghost_two, damage_list, damage_count, parts_mask, parts_strength))
    return from_parts(result)
```

```python
import functools

import jax
import jax.numpy as jnp
from jax import lax
from jax.experimental import pallas as pl
from jax.experimental.pallas import tpu as pltpu
from jax.sharding import PartitionSpec as P

F32, BF16 = jnp.float32, jnp.bfloat16
MESH = pl.DeviceIdType.MESH
OFFSETS = (1, -1, 2, -2)
NQ, NBAS, PAD = 9, 20, 24
ROWS = NQ * PAD
GROUP = 3 * PAD
E, NB = 256, 64
TOP = 112
FRICTION, RELAXATION = 0.6, 0.5


def iota(shape, dim):
    return lax.broadcasted_iota(jnp.int32, shape, dim)


def halves(x):
    hi = x.astype(BF16).astype(F32)
    return hi, x - hi


def right_side(hi, lo):
    rest = jnp.zeros((256 - 3 * GROUP, E), F32)
    return jnp.concatenate([hi, lo, hi, rest], axis=0).astype(BF16)


def dot(a, b):
    return jnp.dot(a, b, preferred_element_type=F32)


def pad_rows(m):
    return jnp.concatenate([m, jnp.zeros((PAD - NBAS, m.shape[1]), F32)], axis=0)


def left_side(mats):
    stacked = jnp.concatenate([pad_rows(m) for m in mats], axis=0)
    hi, lo = halves(stacked)
    lane, row = iota((NBAS, 256), 1), iota((NBAS, 256), 0)
    here = lax.rem(lane, PAD) == row
    one, zero = jnp.ones((NBAS, 256), F32), jnp.zeros((NBAS, 256), F32)
    to_hi = jnp.where(here & (lane < 2 * GROUP), one, zero).astype(BF16)
    to_lo = jnp.where(here & (lane >= 2 * GROUP) & (lane < 3 * GROUP), one, zero).astype(BF16)
    spread = dot(hi.astype(BF16), to_hi) + dot(lo.astype(BF16), to_lo)
    owner = lax.rem(lax.div(iota(spread.shape, 1), PAD), 3)
    blocks = [jnp.where(owner == q, spread, jnp.zeros_like(spread)) for q in range(3)]
    return jnp.concatenate(blocks, axis=0).astype(BF16)


def transposed(m):
    hi, lo = halves(m)
    eye = (iota((NBAS, NBAS), 0) == iota((NBAS, NBAS), 1)).astype(F32).astype(BF16)
    dims = (((1,), (1,)), ((), ()))
    return lax.dot_general(eye, hi.astype(BF16), dims, preferred_element_type=F32) + lax.dot_general(
        eye, lo.astype(BF16), dims, preferred_element_type=F32
    )


def kernel(
    n, dof, star, flux_l, flux_n, kst, f_minus, f_plus, neigh, nface, clus, send_l, dmg, count, ymask, coh, to_p, from_p,
    out, bd_d, bd_o, bd_f, bd_p, coef, onehot, onehot_s, x, x1, st, buf, c1, y, z, ext, ghost, send, recv, ssem, rsem,
):
    me = lax.axis_index("dom")
    barrier = pltpu.get_barrier_semaphore()
    for o in OFFSETS:
        pl.semaphore_signal(barrier, inc=1, device_id=(lax.rem(me + o + n, n),), device_id_type=MESH)

    for q in range(NQ):
        x[PAD * q : PAD * (q + 1), :] = pad_rows(dof[q])

    def widen(q, _):
        for d in range(3):
            coef[d, q] = star[d, q].astype(F32)
        return 0

    lax.fori_loop(0, NQ, widen, 0)
    bd_d[...] = left_side([kst[d] for d in range(3)])
    for j in range(4):
        listed = send_l[0, j : j + 1, :]
        if j % 2 == 0:
            first = listed
        else:
            both = jnp.concatenate([first, listed], axis=1)
            lanes = slice(128 * (j // 2), 128 * (j // 2) + 128)
            onehot_s[:, lanes] = (iota((E, 128), 0) == both).astype(F32).astype(BF16)

    def spread(src, lhs, dst):
        rows = lhs.shape[0]
        for g in range(3):
            dst[rows * g : rows * (g + 1), :] = dot(
                lhs[...], right_side(*halves(src[GROUP * g : GROUP * (g + 1), :]))
            )

    def accumulate(y_ref, row_of, nk, kbase, lanes, accs):
        def step(q, accs):
            accs = list(accs)
            for k in range(nk):
                yv = y_ref[pl.ds(pl.multiple_of(row_of(q, k), 8), PAD), lanes]
                for p in range(NQ):
                    accs[p] = accs[p] + yv * coef[kbase + k, q, p : p + 1, lanes]
            return tuple(accs)

        return lax.fori_loop(0, NQ, step, tuple(accs))

    def zeros9():
        return [jnp.zeros((PAD, 128), F32)] * NQ

    def predictor(src, w1, w2):
        spread(src, bd_d, y)
        for t in range(2):
            lanes = slice(128 * t, 128 * t + 128)
            accs = accumulate(y, lambda q, k: (q * 3 + k) * PAD, 3, 0, lanes, zeros9())
            for p in range(NQ):
                x1[PAD * p : PAD * (p + 1), lanes] = accs[p]
        spread(x1, bd_d, y)
        for t in range(2):
            lanes = slice(128 * t, 128 * t + 128)
            accs = accumulate(y, lambda q, k: (q * 3 + k) * PAD, 3, 0, lanes, zeros9())
            for p in range(NQ):
                rows = slice(PAD * p, PAD * (p + 1))
                buf[rows, lanes] = src[rows, lanes] + w1(lanes) * x1[rows, lanes] + w2(lanes) * accs[p]

    def split_field(field):
        pieces = []
        for g in range(3):
            pieces += list(halves(field[GROUP * g : GROUP * (g + 1), :]))
        return jnp.concatenate(pieces, axis=0).astype(BF16)

    def copies(turn):
        return [
            pltpu.make_async_remote_copy(
                src_ref=send.at[turn, j],
                dst_ref=recv.at[turn, j],
                send_sem=ssem.at[turn, j],
                recv_sem=rsem.at[turn, j],
                device_id=(lax.rem(me + o + n, n),),
                device_id_type=MESH,
            )
            for j, o in enumerate(OFFSETS)
        ]

    low = iota((TOP, 128), 1) < NB

    def start_exchange(turn):
        ext[:, 0:E] = split_field(buf)
        picked = dot(ext[:, 0:E], onehot_s[...])
        packed = jnp.concatenate(
            [picked[2 * GROUP * g : 2 * GROUP * g + GROUP] + picked[2 * GROUP * g + GROUP : 2 * GROUP * (g + 1)] for g in range(3)],
            axis=0,
        )
        for t in range(2):
            upper = packed[0:TOP, 128 * t : 128 * t + 128]
            lower = packed[ROWS - TOP : ROWS, 128 * t : 128 * t + 128]
            send[turn, 2 * t] = jnp.where(low, upper, pltpu.roll(lower, NB, 1))
            send[turn, 2 * t + 1] = jnp.where(low, pltpu.roll(upper, NB, 1), lower)
        for copy in copies(turn):
            copy.start()

    def end_exchange(turn):
        for copy in copies(turn):
            copy.wait_recv()
        for t in range(2):
            one, two = recv[turn, 2 * t], recv[turn, 2 * t + 1]
            lanes = slice(128 * t, 128 * t + 128)
            ghost[0:TOP, lanes] = jnp.where(low, one, pltpu.roll(two, NB, 1))
            ghost[ROWS - TOP : ROWS, lanes] = jnp.where(low, pltpu.roll(one, NB, 1), two)
        ext[:, E : 2 * E] = split_field(ghost)

    def own_side():
        spread(buf, bd_o, y)

    def far_side():
        for f in range(4):
            here = [nface[f : f + 1, :] == h for h in range(3)]
            picked = dot(ext[...], onehot[f])
            for g in range(3):
                hi = picked[2 * GROUP * g : 2 * GROUP * g + GROUP]
                lo = picked[2 * GROUP * g + GROUP : 2 * GROUP * (g + 1)]
                four = dot(bd_f[f], right_side(hi, lo))
                for i in range(3):
                    part = [four[PAD * (4 * i + h) : PAD * (4 * i + h + 1)] for h in range(4)]
                    chosen = jnp.where(here[0], part[0], jnp.where(here[1], part[1], jnp.where(here[2], part[2], part[3])))
                    row = f * ROWS + (3 * g + i) * PAD
                    z[row : row + PAD, :] = chosen

    def own_sum(lanes):
        return accumulate(y, lambda q, k: (q * 7 + k) * PAD, 7, 0, lanes, zeros9())

    def far_sum(lanes, accs):
        return accumulate(z, lambda q, k: k * ROWS + q * PAD, 4, 7, lanes, accs)

    predictor(x, lambda lanes: 0.5, lambda lanes: 1.0 / 6.0)
    pl.semaphore_wait(barrier, len(OFFSETS))
    start_exchange(0)

    def widen_flux(q, _):
        for f in range(4):
            coef[3 + f, q] = flux_l[f, q].astype(F32)
            coef[7 + f, q] = flux_n[f, q].astype(F32)
        return 0

    lax.fori_loop(0, NQ, widen_flux, 0)
    bd_o[...] = left_side([transposed(kst[d]) for d in range(3)] + [-f_minus[f] for f in range(4)])
    for f in range(4):
        bd_f[f] = left_side([-f_plus[f, h] for h in range(4)])
    bd_p[0] = left_side([to_p[...]])
    bd_p[1] = left_side([from_p[...]])
    for f in range(4):
        wanted = neigh[f : f + 1, :]
        onehot[f, 0:E, :] = (iota((E, E), 0) == wanted).astype(F32).astype(BF16)
        for j, o in enumerate(OFFSETS):
            source = me - o
            inside = (source >= 0) & (source < n)
            base = jnp.where(inside, E + NB * j, -4 * E)
            rows = slice(E + NB * j, E + NB * (j + 1))
            onehot[f, rows, :] = ((iota((NB, E), 0) + base) == wanted).astype(F32).astype(BF16)

    own_side()
    for t in range(2):
        lanes = slice(128 * t, 128 * t + 128)
        accs = own_sum(lanes)
        for p in range(NQ):
            c1[PAD * p : PAD * (p + 1), lanes] = accs[p]
    end_exchange(0)
    far_side()
    for t in range(2):
        lanes = slice(128 * t, 128 * t + 128)
        accs = far_sum(lanes, [c1[PAD * p : PAD * (p + 1), lanes] for p in range(NQ)])
        fine = clus[0:1, lanes] == 0
        for p in range(NQ):
            rows = slice(PAD * p, PAD * (p + 1))
            start = x[rows, lanes]
            total = start + accs[p]
            c1[rows, lanes] = total
            st[rows, lanes] = jnp.where(fine, total, start)

    def weight(fine_one, coarse_one):
        return lambda lanes: jnp.where(clus[0:1, lanes] == 0, F32(fine_one), F32(coarse_one))

    predictor(st, weight(0.5, 1.5), weight(1.0 / 6.0, 7.0 / 6.0))
    start_exchange(1)
    own_side()
    for t in range(2):
        lanes = slice(128 * t, 128 * t + 128)
        accs = own_sum(lanes)
        for p in range(NQ):
            rows = slice(PAD * p, PAD * (p + 1))
            c1[rows, lanes] = c1[rows, lanes] + accs[p]
    listed = (iota((E, E), 0) == dmg[...]) & (iota((E, E), 1) < count[0])
    live = lax.dot_general(
        jnp.ones((8, E), BF16), listed.astype(F32).astype(BF16), (((1,), (1,)), ((), ())), preferred_element_type=F32
    )[0:1]
    end_exchange(1)
    far_side()
    for t in range(2):
        lanes = slice(128 * t, 128 * t + 128)
        accs = far_sum(lanes, [c1[PAD * p : PAD * (p + 1), lanes] for p in range(NQ)])
        for p in range(NQ):
            c1[PAD * p : PAD * (p + 1), lanes] = accs[p]

    points = []
    for g in range(2):
        got = dot(bd_p[0], right_side(*halves(c1[GROUP * g : GROUP * (g + 1), :])))
        points += [got[PAD * i : PAD * (i + 1)] for i in range(3)]
    pressure = (points[0] + points[1] + points[2]) / 3.0
    dev = [points[i] - pressure for i in range(3)] + points[3:]
    tau = jnp.sqrt(
        0.5 * (dev[0] * dev[0] + dev[1] * dev[1] + dev[2] * dev[2])
        + (dev[3] * dev[3] + dev[4] * dev[4] + dev[5] * dev[5])
    )
    strength = coh[0:1, :]
    limit = jnp.maximum(strength - FRICTION * pressure, 0.5 * strength)
    rate = RELAXATION * (limit / jnp.maximum(tau, limit) - 1.0)
    marked = jnp.concatenate([ymask[...], jnp.zeros((PAD - NBAS, E), jnp.int32)], axis=0)
    rate = jnp.where((marked == 1) & (live > 0.5), rate, jnp.zeros_like(rate))
    for g in range(2):
        change = jnp.concatenate([rate * dev[3 * g + i] for i in range(3)], axis=0)
        got = dot(bd_p[1], right_side(*halves(change)))
        for i in range(3):
            q = 3 * g + i
            out[q] = c1[PAD * q : PAD * q + NBAS, :] + got[PAD * i : PAD * i + NBAS]
    for q in range(6, NQ):
        out[q] = c1[PAD * q : PAD * q + NBAS, :]
    for turn in range(2):
        for copy in copies(turn):
            copy.wait_send()


def per_device(n, dof, star, flux_l, flux_n, kst, fm, fp, neigh, nface, clus, send_l, dmg, count, ymask, coh, to_p, from_p):
    vmem = pl.BlockSpec(memory_space=pltpu.VMEM)
    smem = pl.BlockSpec(memory_space=pltpu.SMEM)
    return pl.pallas_call(
        functools.partial(kernel, n),
        out_shape=jax.ShapeDtypeStruct((NQ, NBAS, E), F32),
        in_specs=[vmem] * 12 + [smem] + [vmem] * 4,
        out_specs=vmem,
        scratch_shapes=[
            pltpu.VMEM((3 * GROUP, 256), BF16),
            pltpu.VMEM((7 * GROUP, 256), BF16),
            pltpu.VMEM((4, 4 * GROUP, 256), BF16),
            pltpu.VMEM((2, GROUP, 256), BF16),
            pltpu.VMEM((11, NQ, NQ, E), F32),
            pltpu.VMEM((4, 2 * E, E), BF16),
            pltpu.VMEM((E, E), BF16),
            pltpu.VMEM((ROWS, E), F32),
            pltpu.VMEM((ROWS, E), F32),
            pltpu.VMEM((ROWS, E), F32),
            pltpu.VMEM((ROWS, E), F32),
            pltpu.VMEM((ROWS, E), F32),
            pltpu.VMEM((7 * ROWS, E), F32),
            pltpu.VMEM((4 * ROWS, E), F32),
            pltpu.VMEM((2 * ROWS, 2 * E), BF16),
            pltpu.VMEM((ROWS, E), F32),
            pltpu.VMEM((2, 4, TOP, 128), F32),
            pltpu.VMEM((2, 4, TOP, 128), F32),
            pltpu.SemaphoreType.DMA((2, 4)),
            pltpu.SemaphoreType.DMA((2, 4)),
        ],
        compiler_params=pltpu.CompilerParams(
            collective_id=0, has_side_effects=True, vmem_limit_bytes=40 << 20
        ),
        name="ader_cycle",
    )(dof, star, flux_l, flux_n, kst, fm, fp, neigh, nface, clus.reshape(1, E), send_l, dmg, count, ymask, coh.reshape(1, E), to_p, from_p)


def solution(mesh):
    n = mesh.shape["dom"]
    return jax.shard_map(
        functools.partial(per_device, n),
        mesh=mesh,
        in_specs=(
            P(None, None, "dom"),
            P(None, None, None, "dom"),
            P(None, None, None, "dom"),
            P(None, None, None, "dom"),
            P(),
            P(),
            P(),
            P(None, "dom"),
            P(None, "dom"),
            P("dom"),
            P("dom", None, None),
            P("dom", None),
            P("dom"),
            P(None, "dom"),
            P("dom"),
            P(),
            P(),
        ),
        out_specs=P(None, None, "dom"),
        check_vma=False,
    )
```

```python
import functools

import jax
import jax.numpy as jnp
from jax import lax
from jax.experimental import pallas as pl
from jax.experimental.pallas import tpu as pltpu
from jax.sharding import PartitionSpec as P

F32, BF16 = jnp.float32, jnp.bfloat16
MESH = pl.DeviceIdType.MESH
OFFSETS = (1, -1, 2, -2)
NQ, NBAS, PAD = 9, 20, 24
ROWS = NQ * PAD
GROUP = 3 * PAD
E, NB = 256, 64
TOP = 112
FRICTION, RELAXATION = 0.6, 0.5


def iota(shape, dim):
    return lax.broadcasted_iota(jnp.int32, shape, dim)


def halves(x):
    hi = x.astype(BF16).astype(F32)
    return hi, x - hi


def right_side(hi, lo):
    rest = jnp.zeros((256 - 3 * GROUP, E), F32)
    return jnp.concatenate([hi, lo, hi, rest], axis=0).astype(BF16)


def dot(a, b):
    return jnp.dot(a, b, preferred_element_type=F32)


def pad_rows(m):
    return jnp.concatenate([m, jnp.zeros((PAD - NBAS, m.shape[1]), F32)], axis=0)


def left_side(mats):
    stacked = jnp.concatenate([pad_rows(m) for m in mats], axis=0)
    hi, lo = halves(stacked)
    lane, row = iota((NBAS, 256), 1), iota((NBAS, 256), 0)
    here = lax.rem(lane, PAD) == row
    one, zero = jnp.ones((NBAS, 256), F32), jnp.zeros((NBAS, 256), F32)
    to_hi = jnp.where(here & (lane < 2 * GROUP), one, zero).astype(BF16)
    to_lo = jnp.where(here & (lane >= 2 * GROUP) & (lane < 3 * GROUP), one, zero).astype(BF16)
    spread = dot(hi.astype(BF16), to_hi) + dot(lo.astype(BF16), to_lo)
    owner = lax.rem(lax.div(iota(spread.shape, 1), PAD), 3)
    blocks = [jnp.where(owner == q, spread, jnp.zeros_like(spread)) for q in range(3)]
    return jnp.concatenate(blocks, axis=0).astype(BF16)


def transposed(m):
    hi, lo = halves(m)
    eye = (iota((NBAS, NBAS), 0) == iota((NBAS, NBAS), 1)).astype(F32).astype(BF16)
    dims = (((1,), (1,)), ((), ()))
    return lax.dot_general(eye, hi.astype(BF16), dims, preferred_element_type=F32) + lax.dot_general(
        eye, lo.astype(BF16), dims, preferred_element_type=F32
    )


def kernel(
    n, h_dof, h_star, h_flux_l, h_flux_n, h_kst, h_minus, h_plus, h_neigh, h_nface, h_clus, h_send, h_dmg, h_count, h_ymask, h_coh,
    h_to, h_from, out,
    dof, star, flux_l, flux_n, kst, f_minus, f_plus, neigh, nface, clus, send_l, dmg, ymask, coh, to_p, from_p, isem,
    bd_d, bd_o, bd_f, bd_p, coef_s, coef_l, coef_n, onehot, onehot_s, x, x1, st, buf, c1, y, z, ext, ghost, send, recv, ssem, rsem,
):
    me = lax.axis_index("dom")
    pairs = (
        (h_dof, dof), (h_kst, kst), (h_star, star), (h_send, send_l), (h_plus, f_plus), (h_minus, f_minus), (h_flux_l, flux_l),
        (h_flux_n, flux_n), (h_neigh, neigh), (h_nface, nface), (h_clus, clus), (h_to, to_p), (h_from, from_p),
        (h_dmg, dmg), (h_ymask, ymask), (h_coh, coh),
    )
    loads = [pltpu.make_async_copy(src, ref, isem.at[i]) for i, (src, ref) in enumerate(pairs)]
    for load in loads:
        load.start()

    def arrived(*refs):
        for ref in refs:
            for (_, held), load in zip(pairs, loads):
                if held is ref:
                    load.wait()

    def inside(device):
        return (device >= 0) & (device < n)

    barrier = pltpu.get_barrier_semaphore()
    for o in OFFSETS:

        @pl.when(inside(me + o))
        def _():
            pl.semaphore_signal(barrier, inc=1, device_id=(me + o,), device_id_type=MESH)

    partners = sum(jnp.where(inside(me + o), 1, 0) for o in OFFSETS)
    for j, o in enumerate(OFFSETS):

        @pl.when(jnp.logical_not(inside(me - o)))
        def _():
            for turn in range(2):
                recv[turn, j] = jnp.zeros((TOP, 128), F32)

    arrived(dof, kst, star)
    for q in range(NQ):
        x[PAD * q : PAD * (q + 1), :] = pad_rows(dof[q])

    def widen(q, _):
        coef_s[q] = star[q].astype(F32)
        return 0

    lax.fori_loop(0, NQ, widen, 0)
    bd_d[...] = left_side([kst[d] for d in range(3)])
    arrived(send_l)
    for j in range(4):
        listed = send_l[0, j : j + 1, :]
        if j % 2 == 0:
            first = listed
        else:
            both = jnp.concatenate([first, listed], axis=1)
            lanes = slice(128 * (j // 2), 128 * (j // 2) + 128)
            onehot_s[:, lanes] = (iota((E, 128), 0) == both).astype(F32).astype(BF16)

    def spread(src, lhs, dst):
        rows = lhs.shape[0]
        for g in range(3):
            dst[rows * g : rows * (g + 1), :] = dot(
                lhs[...], right_side(*halves(src[GROUP * g : GROUP * (g + 1), :]))
            )

    def accumulate(y_ref, row_of, coefs, lanes, accs):
        def step(q, accs):
            accs = list(accs)
            for k, (coef, i) in enumerate(coefs):
                yv = y_ref[pl.ds(pl.multiple_of(row_of(q, k), 8), PAD), lanes]
                for p in range(NQ):
                    accs[p] = accs[p] + yv * coef[q, p, i : i + 1, lanes]
            return tuple(accs)

        return lax.fori_loop(0, NQ, step, tuple(accs))

    star_coefs = [(coef_s, d) for d in range(3)]
    own_coefs = star_coefs + [(coef_l, f) for f in range(4)]
    far_coefs = [(coef_n, f) for f in range(4)]

    def zeros9():
        return [jnp.zeros((PAD, 128), F32)] * NQ

    def predictor(src, w1, w2):
        spread(src, bd_d, y)
        for t in range(2):
            lanes = slice(128 * t, 128 * t + 128)
            accs = accumulate(y, lambda q, k: (q * 3 + k) * PAD, star_coefs, lanes, zeros9())
            for p in range(NQ):
                x1[PAD * p : PAD * (p + 1), lanes] = accs[p]
        spread(x1, bd_d, y)
        for t in range(2):
            lanes = slice(128 * t, 128 * t + 128)
            accs = accumulate(y, lambda q, k: (q * 3 + k) * PAD, star_coefs, lanes, zeros9())
            for p in range(NQ):
                rows = slice(PAD * p, PAD * (p + 1))
                buf[rows, lanes] = src[rows, lanes] + w1(lanes) * x1[rows, lanes] + w2(lanes) * accs[p]

    def split_field(field):
        pieces = []
        for g in range(3):
            pieces += list(halves(field[GROUP * g : GROUP * (g + 1), :]))
        return jnp.concatenate(pieces, axis=0).astype(BF16)

    def exchange(turn, j):
        return pltpu.make_async_remote_copy(
            src_ref=send.at[turn, j],
            dst_ref=recv.at[turn, j],
            send_sem=ssem.at[turn, j],
            recv_sem=rsem.at[turn, j],
            device_id=(me + OFFSETS[j],),
            device_id_type=MESH,
        )

    def each(act, turn, sign):
        for j, o in enumerate(OFFSETS):

            @pl.when(inside(me + sign * o))
            def _():
                act(exchange(turn, j))

    low = iota((TOP, 128), 1) < NB

    def start_exchange(turn):
        ext[:, 0:E] = split_field(buf)
        picked = dot(ext[:, 0:E], onehot_s[...])
        packed = jnp.concatenate(
            [picked[2 * GROUP * g : 2 * GROUP * g + GROUP] + picked[2 * GROUP * g + GROUP : 2 * GROUP * (g + 1)] for g in range(3)],
            axis=0,
        )
        for t in range(2):
            upper = packed[0:TOP, 128 * t : 128 * t + 128]
            lower = packed[ROWS - TOP : ROWS, 128 * t : 128 * t + 128]
            send[turn, 2 * t] = jnp.where(low, upper, pltpu.roll(lower, NB, 1))
            send[turn, 2 * t + 1] = jnp.where(low, pltpu.roll(upper, NB, 1), lower)
        each(lambda copy: copy.start(), turn, 1)

    def end_exchange(turn):
        each(lambda copy: copy.wait_recv(), turn, -1)
        for t in range(2):
            one, two = recv[turn, 2 * t], recv[turn, 2 * t + 1]
            lanes = slice(128 * t, 128 * t + 128)
            ghost[0:TOP, lanes] = jnp.where(low, one, pltpu.roll(two, NB, 1))
            ghost[ROWS - TOP : ROWS, lanes] = jnp.where(low, pltpu.roll(one, NB, 1), two)
        ext[:, E : 2 * E] = split_field(ghost)

    def own_side():
        spread(buf, bd_o, y)

    def far_side():
        for f in range(4):
            here = [nface[f : f + 1, :] == h for h in range(3)]
            picked = dot(ext[...], onehot[f])
            for g in range(3):
                hi = picked[2 * GROUP * g : 2 * GROUP * g + GROUP]
                lo = picked[2 * GROUP * g + GROUP : 2 * GROUP * (g + 1)]
                four = dot(bd_f[f], right_side(hi, lo))
                for i in range(3):
                    part = [four[PAD * (4 * i + h) : PAD * (4 * i + h + 1)] for h in range(4)]
                    chosen = jnp.where(here[0], part[0], jnp.where(here[1], part[1], jnp.where(here[2], part[2], part[3])))
                    row = f * ROWS + (3 * g + i) * PAD
                    z[row : row + PAD, :] = chosen

    def own_sum(lanes):
        return accumulate(y, lambda q, k: (q * 7 + k) * PAD, own_coefs, lanes, zeros9())

    def far_sum(lanes, accs):
        return accumulate(z, lambda q, k: k * ROWS + q * PAD, far_coefs, lanes, accs)

    predictor(x, lambda lanes: 0.5, lambda lanes: 1.0 / 6.0)
    pl.semaphore_wait(barrier, partners)
    start_exchange(0)
    arrived(f_plus, f_minus, flux_l, flux_n, neigh, nface, clus, to_p, from_p)

    def widen_flux(q, _):
        coef_l[q] = flux_l[q].astype(F32)
        coef_n[q] = flux_n[q].astype(F32)
        return 0

    lax.fori_loop(0, NQ, widen_flux, 0)
    bd_o[...] = left_side([transposed(kst[d]) for d in range(3)] + [-f_minus[:, f, :] for f in range(4)])
    for f in range(4):
        bd_f[f] = left_side([-f_plus[f, :, h, :] for h in range(4)])
    bd_p[0] = left_side([to_p[...]])
    bd_p[1] = left_side([from_p[...]])
    for f in range(4):
        wanted = neigh[f : f + 1, :]
        onehot[f, 0:E, :] = (iota((E, E), 0) == wanted).astype(F32).astype(BF16)
        for j in range(4):
            rows = slice(E + NB * j, E + NB * (j + 1))
            onehot[f, rows, :] = ((iota((NB, E), 0) + E + NB * j) == wanted).astype(F32).astype(BF16)

    own_side()
    for t in range(2):
        lanes = slice(128 * t, 128 * t + 128)
        accs = own_sum(lanes)
        for p in range(NQ):
            c1[PAD * p : PAD * (p + 1), lanes] = accs[p]
    end_exchange(0)
    far_side()
    for t in range(2):
        lanes = slice(128 * t, 128 * t + 128)
        accs = far_sum(lanes, [c1[PAD * p : PAD * (p + 1), lanes] for p in range(NQ)])
        fine = clus[0:1, lanes] == 0
        for p in range(NQ):
            rows = slice(PAD * p, PAD * (p + 1))
            start = x[rows, lanes]
            total = start + accs[p]
            c1[rows, lanes] = total
            st[rows, lanes] = jnp.where(fine, total, start)

    def weight(fine_one, coarse_one):
        return lambda lanes: jnp.where(clus[0:1, lanes] == 0, F32(fine_one), F32(coarse_one))

    predictor(st, weight(0.5, 1.5), weight(1.0 / 6.0, 7.0 / 6.0))
    start_exchange(1)
    own_side()
    for t in range(2):
        lanes = slice(128 * t, 128 * t + 128)
        accs = own_sum(lanes)
        for p in range(NQ):
            rows = slice(PAD * p, PAD * (p + 1))
            c1[rows, lanes] = c1[rows, lanes] + accs[p]
    arrived(dmg, ymask, coh)
    listed = (iota((E, E), 0) == dmg[...]) & (iota((E, E), 1) < h_count[...])
    live = lax.dot_general(
        jnp.ones((8, E), BF16), listed.astype(F32).astype(BF16), (((1,), (1,)), ((), ())), preferred_element_type=F32
    )[0:1]
    end_exchange(1)
    far_side()
    for t in range(2):
        lanes = slice(128 * t, 128 * t + 128)
        accs = far_sum(lanes, [c1[PAD * p : PAD * (p + 1), lanes] for p in range(NQ)])
        for p in range(NQ):
            c1[PAD * p : PAD * (p + 1), lanes] = accs[p]

    points = []
    for g in range(2):
        got = dot(bd_p[0], right_side(*halves(c1[GROUP * g : GROUP * (g + 1), :])))
        points += [got[PAD * i : PAD * (i + 1)] for i in range(3)]
    pressure = (points[0] + points[1] + points[2]) / 3.0
    dev = [points[i] - pressure for i in range(3)] + points[3:]
    tau = jnp.sqrt(
        0.5 * (dev[0] * dev[0] + dev[1] * dev[1] + dev[2] * dev[2])
        + (dev[3] * dev[3] + dev[4] * dev[4] + dev[5] * dev[5])
    )
    strength = coh[0:1, :]
    limit = jnp.maximum(strength - FRICTION * pressure, 0.5 * strength)
    rate = RELAXATION * (limit / jnp.maximum(tau, limit) - 1.0)
    marked = jnp.concatenate([ymask[...], jnp.zeros((PAD - NBAS, E), jnp.int32)], axis=0)
    rate = jnp.where((marked == 1) & (live > 0.5), rate, jnp.zeros_like(rate))
    for g in range(2):
        change = jnp.concatenate([rate * dev[3 * g + i] for i in range(3)], axis=0)
        got = dot(bd_p[1], right_side(*halves(change)))
        for i in range(3):
            q = 3 * g + i
            out[q] = c1[PAD * q : PAD * q + NBAS, :] + got[PAD * i : PAD * i + NBAS]
    for q in range(6, NQ):
        out[q] = c1[PAD * q : PAD * q + NBAS, :]
    for turn in range(2):
        each(lambda copy: copy.wait_send(), turn, 1)


def per_device(n, dof, star, flux_l, flux_n, kst, fm, fp, neigh, nface, clus, send_l, dmg, count, ymask, coh, to_p, from_p):
    operands = (dof, *(jnp.transpose(a, (1, 2, 0, 3)) for a in (star, flux_l, flux_n)), kst, jnp.transpose(fm, (1, 0, 2)), jnp.transpose(fp, (0, 2, 1, 3)), neigh, nface, clus.reshape(1, E), send_l, dmg, count.reshape(1, 1), ymask, coh.reshape(1, E), to_p, from_p)
    hbm = pl.BlockSpec(memory_space=pltpu.HBM)
    vmem = pl.BlockSpec(memory_space=pltpu.VMEM)
    return pl.pallas_call(
        functools.partial(kernel, n),
        out_shape=jax.ShapeDtypeStruct((NQ, NBAS, E), F32),
        in_specs=[hbm] * 12 + [vmem] + [hbm] * 4,
        out_specs=vmem,
        scratch_shapes=[
            pltpu.VMEM((NQ, NBAS, E), F32),
            pltpu.VMEM((NQ, NQ, 3, E), BF16),
            pltpu.VMEM((NQ, NQ, 4, E), BF16),
            pltpu.VMEM((NQ, NQ, 4, E), BF16),
            pltpu.VMEM((3, NBAS, NBAS), F32),
            pltpu.VMEM((NBAS, 4, NBAS), F32),
            pltpu.VMEM((4, NBAS, 4, NBAS), F32),
            pltpu.VMEM((4, E), jnp.int32),
            pltpu.VMEM((4, E), jnp.int32),
            pltpu.VMEM((1, E), jnp.int32),
            pltpu.VMEM((1, 4, NB), jnp.int32),
            pltpu.VMEM((1, E), jnp.int32),
            pltpu.VMEM((NBAS, E), jnp.int32),
            pltpu.VMEM((1, E), F32),
            pltpu.VMEM((NBAS, NBAS), F32),
            pltpu.VMEM((NBAS, NBAS), F32),
            pltpu.SemaphoreType.DMA((17,)),
            pltpu.VMEM((3 * GROUP, 256), BF16),
            pltpu.VMEM((7 * GROUP, 256), BF16),
            pltpu.VMEM((4, 4 * GROUP, 256), BF16),
            pltpu.VMEM((2, GROUP, 256), BF16),
            pltpu.VMEM((NQ, NQ, 3, E), F32),
            pltpu.VMEM((NQ, NQ, 4, E), F32),
            pltpu.VMEM((NQ, NQ, 4, E), F32),
            pltpu.VMEM((4, 2 * E, E), BF16),
            pltpu.VMEM((E, E), BF16),
            pltpu.VMEM((ROWS, E), F32),
            pltpu.VMEM((ROWS, E), F32),
            pltpu.VMEM((ROWS, E), F32),
            pltpu.VMEM((ROWS, E), F32),
            pltpu.VMEM((ROWS, E), F32),
            pltpu.VMEM((7 * ROWS, E), F32),
            pltpu.VMEM((4 * ROWS, E), F32),
            pltpu.VMEM((2 * ROWS, 2 * E), BF16),
            pltpu.VMEM((ROWS, E), F32),
            pltpu.VMEM((2, 4, TOP, 128), F32),
            pltpu.VMEM((2, 4, TOP, 128), F32),
            pltpu.SemaphoreType.DMA((2, 4)),
            pltpu.SemaphoreType.DMA((2, 4)),
        ],
        compiler_params=pltpu.CompilerParams(
            collective_id=0, has_side_effects=True, vmem_limit_bytes=48 << 20
        ),
        name="ader_cycle",
    )(*(a if a.size == 1 else pltpu.with_memory_space_constraint(a, pltpu.HBM) for a in operands))


def solution(mesh):
    n = mesh.shape["dom"]
    return jax.shard_map(
        functools.partial(per_device, n),
        mesh=mesh,
        in_specs=(
            P(None, None, "dom"),
            P(None, None, None, "dom"),
            P(None, None, None, "dom"),
            P(None, None, None, "dom"),
            P(),
            P(),
            P(),
            P(None, "dom"),
            P(None, "dom"),
            P("dom"),
            P("dom", None, None),
            P("dom", None),
            P("dom"),
            P(None, "dom"),
            P("dom"),
            P(),
            P(),
        ),
        out_specs=P(None, None, "dom"),
        check_vma=False,
    )
```

```python
import functools

import jax
import jax.numpy as jnp
from jax import lax
from jax.experimental import pallas as pl
from jax.experimental.pallas import tpu as pltpu
from jax.sharding import PartitionSpec as P

F32, BF16 = jnp.float32, jnp.bfloat16
MESH = pl.DeviceIdType.MESH
OFFSETS = (1, -1, 2, -2)
NQ, NBAS, PAD = 9, 20, 24
ROWS = NQ * PAD
GROUP = 3 * PAD
E, NB = 256, 64
TOP = 112
FRICTION, RELAXATION = 0.6, 0.5


def iota(shape, dim):
    return lax.broadcasted_iota(jnp.int32, shape, dim)


def halves(x):
    hi = x.astype(BF16).astype(F32)
    return hi, x - hi


def right_side(hi, lo):
    rest = jnp.zeros((256 - 3 * GROUP, E), F32)
    return jnp.concatenate([hi, lo, hi, rest], axis=0).astype(BF16)


def dot(a, b):
    return jnp.dot(a, b, preferred_element_type=F32)


def pad_rows(m):
    return jnp.concatenate([m, jnp.zeros((PAD - NBAS, m.shape[1]), F32)], axis=0)


def left_side(mats):
    stacked = jnp.concatenate([pad_rows(m) for m in mats], axis=0)
    hi, lo = halves(stacked)
    lane, row = iota((NBAS, 256), 1), iota((NBAS, 256), 0)
    here = lax.rem(lane, PAD) == row
    one, zero = jnp.ones((NBAS, 256), F32), jnp.zeros((NBAS, 256), F32)
    to_hi = jnp.where(here & (lane < 2 * GROUP), one, zero).astype(BF16)
    to_lo = jnp.where(here & (lane >= 2 * GROUP) & (lane < 3 * GROUP), one, zero).astype(BF16)
    spread = dot(hi.astype(BF16), to_hi) + dot(lo.astype(BF16), to_lo)
    owner = lax.rem(lax.div(iota(spread.shape, 1), PAD), 3)
    blocks = [jnp.where(owner == q, spread, jnp.zeros_like(spread)) for q in range(3)]
    return jnp.concatenate(blocks, axis=0).astype(BF16)


def transposed(m):
    hi, lo = halves(m)
    eye = (iota((NBAS, NBAS), 0) == iota((NBAS, NBAS), 1)).astype(F32).astype(BF16)
    dims = (((1,), (1,)), ((), ()))
    return lax.dot_general(eye, hi.astype(BF16), dims, preferred_element_type=F32) + lax.dot_general(
        eye, lo.astype(BF16), dims, preferred_element_type=F32
    )


def kernel(
    n, h_dof, h_star, h_flux_l, h_flux_n, h_kst, h_minus, h_plus, h_neigh, h_nface, h_clus, h_send, h_dmg, h_count, h_ymask, h_coh,
    h_to, h_from, out,
    dof, star, flux_l, flux_n, kst, f_minus, f_plus, neigh, nface, clus, send_l, dmg, ymask, coh, to_p, from_p, isem,
    bd_d, bd_o, bd_f, bd_p, coef_s, coef_l, coef_n, onehot, onehot_s, x, x1, st, buf, c1, part, y, z, ext, near, ghost, send, recv, ssem, rsem,
):
    me = lax.axis_index("dom")
    pairs = (
        (h_dof, dof), (h_kst, kst), (h_star, star), (h_send, send_l), (h_plus, f_plus), (h_minus, f_minus), (h_flux_l, flux_l),
        (h_flux_n, flux_n), (h_neigh, neigh), (h_nface, nface), (h_clus, clus), (h_to, to_p), (h_from, from_p),
        (h_dmg, dmg), (h_ymask, ymask), (h_coh, coh),
    )
    loads = [pltpu.make_async_copy(src, ref, isem.at[i]) for i, (src, ref) in enumerate(pairs)]
    for load in loads:
        load.start()

    def arrived(*refs):
        for ref in refs:
            for (_, held), load in zip(pairs, loads):
                if held is ref:
                    load.wait()

    def inside(device):
        return (device >= 0) & (device < n)

    barrier = pltpu.get_barrier_semaphore()
    for o in OFFSETS:

        @pl.when(inside(me + o))
        def _():
            pl.semaphore_signal(barrier, inc=1, device_id=(me + o,), device_id_type=MESH)

    partners = sum(jnp.where(inside(me + o), 1, 0) for o in OFFSETS)
    for j, o in enumerate(OFFSETS):

        @pl.when(jnp.logical_not(inside(me - o)))
        def _():
            for turn in range(2):
                recv[turn, j] = jnp.zeros((TOP, 128), F32)

    arrived(dof, kst, star)
    for q in range(NQ):
        x[PAD * q : PAD * (q + 1), :] = pad_rows(dof[q])

    def widen(q, _):
        coef_s[q] = star[q].astype(F32)
        return 0

    lax.fori_loop(0, NQ, widen, 0)
    bd_d[...] = left_side([kst[d] for d in range(3)])
    arrived(send_l)
    for j in range(4):
        listed = send_l[0, j : j + 1, :]
        if j % 2 == 0:
            first = listed
        else:
            both = jnp.concatenate([first, listed], axis=1)
            lanes = slice(128 * (j // 2), 128 * (j // 2) + 128)
            onehot_s[:, lanes] = (iota((E, 128), 0) == both).astype(F32).astype(BF16)

    def tiles():
        return [slice(0, 128), slice(128, 256)]

    def spread(src, lhs, dst, g):
        rows = lhs.shape[0]
        dst[rows * g : rows * (g + 1), :] = dot(lhs[...], right_side(*halves(src[GROUP * g : GROUP * (g + 1), :])))

    def accumulate(y_ref, row_of, coefs, quantities, lanes, accs):
        accs = list(accs)
        for q in quantities:
            for k, (coef, i) in enumerate(coefs):
                yv = y_ref[row_of(q, k) : row_of(q, k) + PAD, lanes]
                for p in range(NQ):
                    term = yv * coef[q, p, i : i + 1, lanes]
                    accs[p] = term if accs[p] is None else accs[p] + term
        return accs

    def held(ref, lanes):
        return [ref[PAD * p : PAD * (p + 1), lanes] for p in range(NQ)]

    def hold(ref, lanes, accs):
        for p in range(NQ):
            ref[PAD * p : PAD * (p + 1), lanes] = accs[p]

    def grouped(src, lhs, coefs, finish):
        nk = len(coefs)
        spread(src, lhs, y, 0)
        for g in range(3):
            if g < 2:
                spread(src, lhs, y, g + 1)
            for lanes in tiles():
                accs = [None] * NQ if g == 0 else held(part, lanes)
                accs = accumulate(y, lambda q, k: (q * nk + k) * PAD, coefs, range(3 * g, 3 * g + 3), lanes, accs)
                if g < 2:
                    hold(part, lanes, accs)
                else:
                    finish(lanes, accs)

    star_coefs = [(coef_s, d) for d in range(3)]
    own_coefs = star_coefs + [(coef_l, f) for f in range(4)]

    def predictor(src, w1, w2):
        grouped(src, bd_d, star_coefs, functools.partial(hold, x1))

        def finish(lanes, accs):
            for p in range(NQ):
                rows = slice(PAD * p, PAD * (p + 1))
                buf[rows, lanes] = src[rows, lanes] + w1(lanes) * x1[rows, lanes] + w2(lanes) * accs[p]

        grouped(x1, bd_d, star_coefs, finish)

    def split_field(field):
        pieces = []
        for g in range(3):
            pieces += list(halves(field[GROUP * g : GROUP * (g + 1), :]))
        return jnp.concatenate(pieces, axis=0).astype(BF16)

    def exchange(turn, j):
        return pltpu.make_async_remote_copy(
            src_ref=send.at[turn, j],
            dst_ref=recv.at[turn, j],
            send_sem=ssem.at[turn, j],
            recv_sem=rsem.at[turn, j],
            device_id=(me + OFFSETS[j],),
            device_id_type=MESH,
        )

    def each(act, turn, sign):
        for j, o in enumerate(OFFSETS):

            @pl.when(inside(me + sign * o))
            def _():
                act(exchange(turn, j))

    low = iota((TOP, 128), 1) < NB

    def start_exchange(turn):
        ext[:, 0:E] = split_field(buf)
        picked = dot(ext[:, 0:E], onehot_s[...])
        packed = jnp.concatenate(
            [picked[2 * GROUP * g : 2 * GROUP * g + GROUP] + picked[2 * GROUP * g + GROUP : 2 * GROUP * (g + 1)] for g in range(3)],
            axis=0,
        )
        for t in range(2):
            upper = packed[0:TOP, 128 * t : 128 * t + 128]
            lower = packed[ROWS - TOP : ROWS, 128 * t : 128 * t + 128]
            send[turn, 2 * t] = jnp.where(low, upper, pltpu.roll(lower, NB, 1))
            send[turn, 2 * t + 1] = jnp.where(low, pltpu.roll(upper, NB, 1), lower)
        each(lambda copy: copy.start(), turn, 1)

    def end_exchange(turn):
        each(lambda copy: copy.wait_recv(), turn, -1)
        for t in range(2):
            one, two = recv[turn, 2 * t], recv[turn, 2 * t + 1]
            lanes = slice(128 * t, 128 * t + 128)
            ghost[0:TOP, lanes] = jnp.where(low, one, pltpu.roll(two, NB, 1))
            ghost[ROWS - TOP : ROWS, lanes] = jnp.where(low, pltpu.roll(one, NB, 1), two)
        ext[:, E : 2 * E] = split_field(ghost)

    def own_side(finish):
        grouped(buf, bd_o, own_coefs, finish)

    def near_picks():
        for f in range(4):
            near[f] = dot(ext[:, 0:E], onehot[f, 0:E, :]).astype(BF16)

    def face(f):
        here = [nface[f : f + 1, :] == h for h in range(3)]
        picked = dot(ext[...], onehot[f])
        for g in range(3):
            hi = picked[2 * GROUP * g : 2 * GROUP * g + GROUP]
            lo = picked[2 * GROUP * g + GROUP : 2 * GROUP * (g + 1)]
            four = dot(bd_f[f], right_side(hi, lo))
            for i in range(3):
                part_h = [four[PAD * (4 * i + h) : PAD * (4 * i + h + 1)] for h in range(4)]
                row = f * ROWS + (3 * g + i) * PAD
                z[row : row + PAD, :] = jnp.where(
                    here[0], part_h[0], jnp.where(here[1], part_h[1], jnp.where(here[2], part_h[2], part_h[3]))
                )

    def far_side(finish):
        face(0)
        for f in range(4):
            if f < 3:
                face(f + 1)
            for lanes in tiles():
                accs = accumulate(z, lambda q, k: f * ROWS + q * PAD, [(coef_n, f)], range(NQ), lanes, held(c1, lanes))
                if f < 3:
                    hold(c1, lanes, accs)
                else:
                    finish(lanes, accs)

    predictor(x, lambda lanes: 0.5, lambda lanes: 1.0 / 6.0)
    pl.semaphore_wait(barrier, partners)
    start_exchange(0)
    arrived(f_plus, f_minus, flux_l, flux_n, neigh, nface, clus, to_p, from_p)

    def widen_flux(q, _):
        coef_l[q] = flux_l[q].astype(F32)
        coef_n[q] = flux_n[q].astype(F32)
        return 0

    lax.fori_loop(0, NQ, widen_flux, 0)
    bd_o[...] = left_side([transposed(kst[d]) for d in range(3)] + [-f_minus[:, f, :] for f in range(4)])
    for f in range(4):
        bd_f[f] = left_side([-f_plus[f, :, h, :] for h in range(4)])
    bd_p[0] = left_side([to_p[...]])
    bd_p[1] = left_side([from_p[...]])
    for f in range(4):
        wanted = neigh[f : f + 1, :]
        onehot[f, 0:E, :] = (iota((E, E), 0) == wanted).astype(F32).astype(BF16)
        for j in range(4):
            rows = slice(E + NB * j, E + NB * (j + 1))
            onehot[f, rows, :] = ((iota((NB, E), 0) + E + NB * j) == wanted).astype(F32).astype(BF16)

    own_side(functools.partial(hold, c1))
    end_exchange(0)

    def finish_one(lanes, accs):
        fine = clus[0:1, lanes] == 0
        for p in range(NQ):
            rows = slice(PAD * p, PAD * (p + 1))
            start = x[rows, lanes]
            total = start + accs[p]
            c1[rows, lanes] = total
            st[rows, lanes] = jnp.where(fine, total, start)

    far_side(finish_one)

    def weight(fine_one, coarse_one):
        return lambda lanes: jnp.where(clus[0:1, lanes] == 0, F32(fine_one), F32(coarse_one))

    predictor(st, weight(0.5, 1.5), weight(1.0 / 6.0, 7.0 / 6.0))
    start_exchange(1)

    def finish_two(lanes, accs):
        for p in range(NQ):
            rows = slice(PAD * p, PAD * (p + 1))
            c1[rows, lanes] = c1[rows, lanes] + accs[p]

    own_side(finish_two)
    arrived(dmg, ymask, coh)
    listed = (iota((E, E), 0) == dmg[...]) & (iota((E, E), 1) < h_count[...])
    live = lax.dot_general(
        jnp.ones((8, E), BF16), listed.astype(F32).astype(BF16), (((1,), (1,)), ((), ())), preferred_element_type=F32
    )[0:1]
    end_exchange(1)
    far_side(functools.partial(hold, c1))

    points = []
    for g in range(2):
        got = dot(bd_p[0], right_side(*halves(c1[GROUP * g : GROUP * (g + 1), :])))
        points += [got[PAD * i : PAD * (i + 1)] for i in range(3)]
    pressure = (points[0] + points[1] + points[2]) / 3.0
    dev = [points[i] - pressure for i in range(3)] + points[3:]
    tau = jnp.sqrt(
        0.5 * (dev[0] * dev[0] + dev[1] * dev[1] + dev[2] * dev[2])
        + (dev[3] * dev[3] + dev[4] * dev[4] + dev[5] * dev[5])
    )
    strength = coh[0:1, :]
    limit = jnp.maximum(strength - FRICTION * pressure, 0.5 * strength)
    rate = RELAXATION * (limit / jnp.maximum(tau, limit) - 1.0)
    marked = jnp.concatenate([ymask[...], jnp.zeros((PAD - NBAS, E), jnp.int32)], axis=0)
    rate = jnp.where((marked == 1) & (live > 0.5), rate, jnp.zeros_like(rate))
    for g in range(2):
        change = jnp.concatenate([rate * dev[3 * g + i] for i in range(3)], axis=0)
        got = dot(bd_p[1], right_side(*halves(change)))
        for i in range(3):
            q = 3 * g + i
            out[q] = c1[PAD * q : PAD * q + NBAS, :] + got[PAD * i : PAD * i + NBAS]
    for q in range(6, NQ):
        out[q] = c1[PAD * q : PAD * q + NBAS, :]
    for turn in range(2):
        each(lambda copy: copy.wait_send(), turn, 1)


def per_device(n, dof, star, flux_l, flux_n, kst, fm, fp, neigh, nface, clus, send_l, dmg, count, ymask, coh, to_p, from_p):
    operands = (dof, *(jnp.transpose(a, (1, 2, 0, 3)) for a in (star, flux_l, flux_n)), kst, jnp.transpose(fm, (1, 0, 2)), jnp.transpose(fp, (0, 2, 1, 3)), neigh, nface, clus.reshape(1, E), send_l, dmg, count.reshape(1, 1), ymask, coh.reshape(1, E), to_p, from_p)
    hbm = pl.BlockSpec(memory_space=pltpu.HBM)
    vmem = pl.BlockSpec(memory_space=pltpu.VMEM)
    return pl.pallas_call(
        functools.partial(kernel, n),
        out_shape=jax.ShapeDtypeStruct((NQ, NBAS, E), F32),
        in_specs=[hbm] * 12 + [vmem] + [hbm] * 4,
        out_specs=vmem,
        scratch_shapes=[
            pltpu.VMEM((NQ, NBAS, E), F32),
            pltpu.VMEM((NQ, NQ, 3, E), BF16),
            pltpu.VMEM((NQ, NQ, 4, E), BF16),
            pltpu.VMEM((NQ, NQ, 4, E), BF16),
            pltpu.VMEM((3, NBAS, NBAS), F32),
            pltpu.VMEM((NBAS, 4, NBAS), F32),
            pltpu.VMEM((4, NBAS, 4, NBAS), F32),
            pltpu.VMEM((4, E), jnp.int32),
            pltpu.VMEM((4, E), jnp.int32),
            pltpu.VMEM((1, E), jnp.int32),
            pltpu.VMEM((1, 4, NB), jnp.int32),
            pltpu.VMEM((1, E), jnp.int32),
            pltpu.VMEM((NBAS, E), jnp.int32),
            pltpu.VMEM((1, E), F32),
            pltpu.VMEM((NBAS, NBAS), F32),
            pltpu.VMEM((NBAS, NBAS), F32),
            pltpu.SemaphoreType.DMA((17,)),
            pltpu.VMEM((3 * GROUP, 256), BF16),
            pltpu.VMEM((7 * GROUP, 256), BF16),
            pltpu.VMEM((4, 4 * GROUP, 256), BF16),
            pltpu.VMEM((2, GROUP, 256), BF16),
            pltpu.VMEM((NQ, NQ, 3, E), F32),
            pltpu.VMEM((NQ, NQ, 4, E), F32),
            pltpu.VMEM((NQ, NQ, 4, E), F32),
            pltpu.VMEM((4, 2 * E, E), BF16),
            pltpu.VMEM((E, E), BF16),
            pltpu.VMEM((ROWS, E), F32),
            pltpu.VMEM((ROWS, E), F32),
            pltpu.VMEM((ROWS, E), F32),
            pltpu.VMEM((ROWS, E), F32),
            pltpu.VMEM((ROWS, E), F32),
            pltpu.VMEM((ROWS, E), F32),
            pltpu.VMEM((7 * ROWS, E), F32),
            pltpu.VMEM((4 * ROWS, E), F32),
            pltpu.VMEM((2 * ROWS, 2 * E), BF16),
            pltpu.VMEM((4, 2 * ROWS, E), BF16),
            pltpu.VMEM((ROWS, E), F32),
            pltpu.VMEM((2, 4, TOP, 128), F32),
            pltpu.VMEM((2, 4, TOP, 128), F32),
            pltpu.SemaphoreType.DMA((2, 4)),
            pltpu.SemaphoreType.DMA((2, 4)),
        ],
        compiler_params=pltpu.CompilerParams(
            collective_id=0, has_side_effects=True, vmem_limit_bytes=48 << 20
        ),
        name="ader_cycle",
    )(*(a if a.size == 1 else pltpu.with_memory_space_constraint(a, pltpu.HBM) for a in operands))


def solution(mesh):
    n = mesh.shape["dom"]
    return jax.shard_map(
        functools.partial(per_device, n),
        mesh=mesh,
        in_specs=(
            P(None, None, "dom"),
            P(None, None, None, "dom"),
            P(None, None, None, "dom"),
            P(None, None, None, "dom"),
            P(),
            P(),
            P(),
            P(None, "dom"),
            P(None, "dom"),
            P("dom"),
            P("dom", None, None),
            P("dom", None),
            P("dom"),
            P(None, "dom"),
            P("dom"),
            P(),
            P(),
        ),
        out_specs=P(None, None, "dom"),
        check_vma=False,
    )
```

```python
import functools

import jax
import jax.numpy as jnp
from jax import lax
from jax.experimental import pallas as pl
from jax.experimental.pallas import tpu as pltpu
from jax.sharding import PartitionSpec as P

F32, BF16 = jnp.float32, jnp.bfloat16
MESH = pl.DeviceIdType.MESH
OFFSETS = (1, -1, 2, -2)
NQ, NBAS, PAD = 9, 20, 24
ROWS = NQ * PAD
GROUP = 3 * PAD
E, NB = 256, 64
PAIRS, REST = 4, 12
FRICTION, RELAXATION = 0.6, 0.5


def iota(shape, dim):
    return lax.broadcasted_iota(jnp.int32, shape, dim)


def halves(x):
    hi = x.astype(BF16).astype(F32)
    return hi, x - hi


def right_side(hi, lo):
    rest = jnp.zeros((256 - 3 * GROUP, E), F32)
    return jnp.concatenate([hi, lo, hi, rest], axis=0).astype(BF16)


def dot(a, b):
    return jnp.dot(a, b, preferred_element_type=F32)


def pad_rows(m):
    return jnp.concatenate([m, jnp.zeros((PAD - NBAS, m.shape[1]), F32)], axis=0)


def left_side(mats):
    stacked = jnp.concatenate([pad_rows(m) for m in mats], axis=0)
    hi, lo = halves(stacked)
    lane, row = iota((NBAS, 256), 1), iota((NBAS, 256), 0)
    here = lax.rem(lane, PAD) == row
    one, zero = jnp.ones((NBAS, 256), F32), jnp.zeros((NBAS, 256), F32)
    to_hi = jnp.where(here & (lane < 2 * GROUP), one, zero).astype(BF16)
    to_lo = jnp.where(here & (lane >= 2 * GROUP) & (lane < 3 * GROUP), one, zero).astype(BF16)
    spread = dot(hi.astype(BF16), to_hi) + dot(lo.astype(BF16), to_lo)
    owner = lax.rem(lax.div(iota(spread.shape, 1), PAD), 3)
    blocks = [jnp.where(owner == q, spread, jnp.zeros_like(spread)) for q in range(3)]
    return jnp.concatenate(blocks, axis=0).astype(BF16)


def transposed(m):
    hi, lo = halves(m)
    eye = (iota((NBAS, NBAS), 0) == iota((NBAS, NBAS), 1)).astype(F32).astype(BF16)
    dims = (((1,), (1,)), ((), ()))
    return lax.dot_general(eye, hi.astype(BF16), dims, preferred_element_type=F32) + lax.dot_general(
        eye, lo.astype(BF16), dims, preferred_element_type=F32
    )


def kernel(
    n, h_dof, h_star, h_flux_l, h_flux_n, h_kst, h_minus, h_plus, h_neigh, h_nface, h_clus, h_send, h_dmg, h_count, h_ymask, h_coh,
    h_to, h_from, out,
    dof, star, flux_l, flux_n, kst, f_minus, f_plus, neigh, nface, clus, send_l, dmg, ymask, coh, to_p, from_p, isem,
    bd_d, bd_o, bd_f, bd_p, coef_s, coef_l, coef_n, onehot, onehot_s, x, x1, st, buf, c1, part, y0, y1, y2, z0, z1, z2, z3, ext, near, ghost, send_a, send_b, recv_a, recv_b, ssem, rsem,
):
    me = lax.axis_index("dom")
    y, z = (y0, y1, y2), (z0, z1, z2, z3)
    pairs = (
        (h_dof, dof), (h_kst, kst), (h_star, star), (h_send, send_l), (h_plus, f_plus), (h_minus, f_minus), (h_flux_l, flux_l),
        (h_flux_n, flux_n), (h_neigh, neigh), (h_nface, nface), (h_clus, clus), (h_to, to_p), (h_from, from_p),
        (h_dmg, dmg), (h_ymask, ymask), (h_coh, coh),
    )
    loads = [pltpu.make_async_copy(src, ref, isem.at[i]) for i, (src, ref) in enumerate(pairs)]
    for load in loads:
        load.start()

    def arrived(*refs):
        for ref in refs:
            for (_, held), load in zip(pairs, loads):
                if held is ref:
                    load.wait()

    def inside(device):
        return (device >= 0) & (device < n)

    barrier = pltpu.get_barrier_semaphore()
    for o in OFFSETS:

        @pl.when(inside(me + o))
        def _():
            pl.semaphore_signal(barrier, inc=1, device_id=(me + o,), device_id_type=MESH)

    partners = sum(jnp.where(inside(me + o), 1, 0) for o in OFFSETS)
    for j, o in enumerate(OFFSETS):

        for turn in range(2):
            recv_a[turn, j, :, NBAS:PAD, :] = jnp.zeros((PAIRS, PAD - NBAS, 128), F32)
            recv_b[turn, j, REST:16, :] = jnp.zeros((16 - REST, 128), F32)

        @pl.when(jnp.logical_not(inside(me - o)))
        def _():
            for turn in range(2):
                recv_a[turn, j, :, 0:NBAS, :] = jnp.zeros((PAIRS, NBAS, 128), F32)
                recv_b[turn, j, 0:REST, :] = jnp.zeros((REST, 128), F32)

    arrived(dof, kst, star)
    for q in range(NQ):
        x[PAD * q : PAD * (q + 1), :] = pad_rows(dof[q])

    def widen(q, _):
        coef_s[q] = star[q].astype(F32)
        return 0

    lax.fori_loop(0, NQ, widen, 0)
    bd_d[...] = left_side([kst[d] for d in range(3)])
    arrived(send_l)
    for j in range(4):
        listed = send_l[0, j : j + 1, :]
        if j % 2 == 0:
            first = listed
        else:
            both = jnp.concatenate([first, listed], axis=1)
            lanes = slice(128 * (j // 2), 128 * (j // 2) + 128)
            onehot_s[:, lanes] = (iota((E, 128), 0) == both).astype(F32).astype(BF16)

    def tiles():
        return [slice(0, 128), slice(128, 256)]

    def spread(src, lhs, dst, g):
        rows = lhs.shape[0]
        dst[g][0:rows, :] = dot(lhs[...], right_side(*halves(src[GROUP * g : GROUP * (g + 1), :])))

    def accumulate(y_ref, row_of, coefs, quantities, lanes, accs):
        accs = list(accs)
        for q in quantities:
            for k, (coef, i) in enumerate(coefs):
                yv = y_ref[row_of(q, k) : row_of(q, k) + PAD, lanes]
                for p in range(NQ):
                    term = yv * coef[q, p, i : i + 1, lanes]
                    accs[p] = term if accs[p] is None else accs[p] + term
        return accs

    def held(ref, lanes):
        return [ref[PAD * p : PAD * (p + 1), lanes] for p in range(NQ)]

    def hold(ref, lanes, accs):
        for p in range(NQ):
            ref[PAD * p : PAD * (p + 1), lanes] = accs[p]

    def grouped(src, lhs, coefs, finish):
        nk = len(coefs)
        spread(src, lhs, y, 0)
        for g in range(3):
            if g < 2:
                spread(src, lhs, y, g + 1)
            for lanes in tiles():
                accs = [None] * NQ if g == 0 else held(part, lanes)
                accs = accumulate(y[g], lambda q, k: ((q - 3 * g) * nk + k) * PAD, coefs, range(3 * g, 3 * g + 3), lanes, accs)
                if g < 2:
                    hold(part, lanes, accs)
                else:
                    finish(lanes, accs)

    star_coefs = [(coef_s, d) for d in range(3)]
    own_coefs = star_coefs + [(coef_l, f) for f in range(4)]

    def predictor(src, w1, w2):
        grouped(src, bd_d, star_coefs, functools.partial(hold, x1))

        def finish(lanes, accs):
            for p in range(NQ):
                rows = slice(PAD * p, PAD * (p + 1))
                buf[rows, lanes] = src[rows, lanes] + w1(lanes) * x1[rows, lanes] + w2(lanes) * accs[p]

        grouped(x1, bd_d, star_coefs, finish)

    def split_field(field):
        pieces = []
        for g in range(3):
            pieces += list(halves(field[GROUP * g : GROUP * (g + 1), :]))
        return jnp.concatenate(pieces, axis=0).astype(BF16)

    def exchange(turn, j):
        parts = (
            (send_a.at[turn, j, :, 0:NBAS, :], recv_a.at[turn, j, :, 0:NBAS, :]),
            (send_b.at[turn, j, 0:REST, :], recv_b.at[turn, j, 0:REST, :]),
        )
        return [
            pltpu.make_async_remote_copy(
                src_ref=source,
                dst_ref=target,
                send_sem=ssem.at[turn, j, i],
                recv_sem=rsem.at[turn, j, i],
                device_id=(me + OFFSETS[j],),
                device_id_type=MESH,
            )
            for i, (source, target) in enumerate(parts)
        ]

    def each(act, turn, sign):
        for j, o in enumerate(OFFSETS):

            @pl.when(inside(me + sign * o))
            def _():
                for copy in exchange(turn, j):
                    act(copy)

    low = iota((PAD, 128), 1) < NB

    def swap(one, two):
        mask = low[0 : one.shape[0]]
        return jnp.where(mask, one, pltpu.roll(two, NB, 1)), jnp.where(mask, pltpu.roll(one, NB, 1), two)

    def start_exchange(turn):
        ext[:, 0:E] = split_field(buf)
        picked = dot(ext[:, 0:E], onehot_s[...])
        packed = jnp.concatenate(
            [picked[2 * GROUP * g : 2 * GROUP * g + GROUP] + picked[2 * GROUP * g + GROUP : 2 * GROUP * (g + 1)] for g in range(3)],
            axis=0,
        )
        for t, lanes in enumerate(tiles()):
            for i in range(PAIRS):
                upper = packed[PAD * i : PAD * (i + 1), lanes]
                lower = packed[PAD * (i + PAIRS) : PAD * (i + PAIRS + 1), lanes]
                send_a[turn, 2 * t, i], send_a[turn, 2 * t + 1, i] = swap(upper, lower)
            last = packed[8 * PAD : ROWS, lanes]
            send_b[turn, 2 * t, 0:8, :], send_b[turn, 2 * t + 1, 0:8, :] = swap(last[0:8], last[8:16])
            send_b[turn, 2 * t, 8:16, :], send_b[turn, 2 * t + 1, 8:16, :] = last[16:24], pltpu.roll(last[16:24], NB, 1)
        each(lambda copy: copy.start(), turn, 1)

    def end_exchange(turn):
        each(lambda copy: copy.wait_recv(), turn, -1)
        for t, lanes in enumerate(tiles()):
            for i in range(PAIRS):
                upper, lower = swap(recv_a[turn, 2 * t, i], recv_a[turn, 2 * t + 1, i])
                ghost[PAD * i : PAD * (i + 1), lanes] = upper
                ghost[PAD * (i + PAIRS) : PAD * (i + PAIRS + 1), lanes] = lower
            one, two = recv_b[turn, 2 * t], recv_b[turn, 2 * t + 1]
            upper, lower = swap(one[0:8], two[0:8])
            ghost[8 * PAD : 8 * PAD + 8, lanes] = upper
            ghost[8 * PAD + 8 : 8 * PAD + 16, lanes] = lower
            ghost[8 * PAD + 16 : ROWS, lanes] = swap(one[8:16], two[8:16])[0]
        ext[:, E : 2 * E] = split_field(ghost)

    def own_side(finish):
        grouped(buf, bd_o, own_coefs, finish)

    def near_picks():
        for f in range(4):
            near[f] = dot(ext[:, 0:E], onehot[f, 0:E, :]).astype(BF16)

    def face(f):
        here = [nface[f : f + 1, :] == h for h in range(3)]
        picked = dot(ext[...], onehot[f])
        for g in range(3):
            hi = picked[2 * GROUP * g : 2 * GROUP * g + GROUP]
            lo = picked[2 * GROUP * g + GROUP : 2 * GROUP * (g + 1)]
            four = dot(bd_f[f], right_side(hi, lo))
            for i in range(3):
                part_h = [four[PAD * (4 * i + h) : PAD * (4 * i + h + 1)] for h in range(4)]
                row = (3 * g + i) * PAD
                z[f][row : row + PAD, :] = jnp.where(
                    here[0], part_h[0], jnp.where(here[1], part_h[1], jnp.where(here[2], part_h[2], part_h[3]))
                )

    def far_side(finish):
        for f in range(4):
            face(f)
        for lanes in tiles():
            accs = held(c1, lanes)
            for f in range(4):
                accs = accumulate(z[f], lambda q, k: q * PAD, [(coef_n, f)], range(NQ), lanes, accs)
            finish(lanes, accs)

    predictor(x, lambda lanes: 0.5, lambda lanes: 1.0 / 6.0)
    pl.semaphore_wait(barrier, partners)
    start_exchange(0)
    arrived(f_plus, f_minus, flux_l, flux_n, neigh, nface, clus, to_p, from_p)

    def widen_flux(q, _):
        coef_l[q] = flux_l[q].astype(F32)
        coef_n[q] = flux_n[q].astype(F32)
        return 0

    lax.fori_loop(0, NQ, widen_flux, 0)
    bd_o[...] = left_side([transposed(kst[d]) for d in range(3)] + [-f_minus[:, f, :] for f in range(4)])
    for f in range(4):
        bd_f[f] = left_side([-f_plus[f, :, h, :] for h in range(4)])
    bd_p[0] = left_side([to_p[...]])
    bd_p[1] = left_side([from_p[...]])
    for f in range(4):
        wanted = neigh[f : f + 1, :]
        onehot[f, 0:E, :] = (iota((E, E), 0) == wanted).astype(F32).astype(BF16)
        for j in range(4):
            rows = slice(E + NB * j, E + NB * (j + 1))
            onehot[f, rows, :] = ((iota((NB, E), 0) + E + NB * j) == wanted).astype(F32).astype(BF16)

    own_side(functools.partial(hold, c1))
    end_exchange(0)

    def finish_one(lanes, accs):
        fine = clus[0:1, lanes] == 0
        for p in range(NQ):
            rows = slice(PAD * p, PAD * (p + 1))
            start = x[rows, lanes]
            total = start + accs[p]
            c1[rows, lanes] = total
            st[rows, lanes] = jnp.where(fine, total, start)

    far_side(finish_one)

    def weight(fine_one, coarse_one):
        return lambda lanes: jnp.where(clus[0:1, lanes] == 0, F32(fine_one), F32(coarse_one))

    predictor(st, weight(0.5, 1.5), weight(1.0 / 6.0, 7.0 / 6.0))
    start_exchange(1)

    def finish_two(lanes, accs):
        for p in range(NQ):
            rows = slice(PAD * p, PAD * (p + 1))
            c1[rows, lanes] = c1[rows, lanes] + accs[p]

    own_side(finish_two)
    arrived(dmg, ymask, coh)
    listed = (iota((E, E), 0) == dmg[...]) & (iota((E, E), 1) < h_count[...])
    live = lax.dot_general(
        jnp.ones((8, E), BF16), listed.astype(F32).astype(BF16), (((1,), (1,)), ((), ())), preferred_element_type=F32
    )[0:1]
    end_exchange(1)
    far_side(functools.partial(hold, c1))

    points = []
    for g in range(2):
        got = dot(bd_p[0], right_side(*halves(c1[GROUP * g : GROUP * (g + 1), :])))
        points += [got[PAD * i : PAD * (i + 1)] for i in range(3)]
    pressure = (points[0] + points[1] + points[2]) / 3.0
    dev = [points[i] - pressure for i in range(3)] + points[3:]
    tau = jnp.sqrt(
        0.5 * (dev[0] * dev[0] + dev[1] * dev[1] + dev[2] * dev[2])
        + (dev[3] * dev[3] + dev[4] * dev[4] + dev[5] * dev[5])
    )
    strength = coh[0:1, :]
    limit = jnp.maximum(strength - FRICTION * pressure, 0.5 * strength)
    rate = RELAXATION * (limit / jnp.maximum(tau, limit) - 1.0)
    marked = jnp.concatenate([ymask[...], jnp.zeros((PAD - NBAS, E), jnp.int32)], axis=0)
    rate = jnp.where((marked == 1) & (live > 0.5), rate, jnp.zeros_like(rate))
    for g in range(2):
        change = jnp.concatenate([rate * dev[3 * g + i] for i in range(3)], axis=0)
        got = dot(bd_p[1], right_side(*halves(change)))
        for i in range(3):
            q = 3 * g + i
            out[q] = c1[PAD * q : PAD * q + NBAS, :] + got[PAD * i : PAD * i + NBAS]
    for q in range(6, NQ):
        out[q] = c1[PAD * q : PAD * q + NBAS, :]
    for turn in range(2):
        each(lambda copy: copy.wait_send(), turn, 1)


def per_device(n, dof, star, flux_l, flux_n, kst, fm, fp, neigh, nface, clus, send_l, dmg, count, ymask, coh, to_p, from_p):
    operands = (dof, *(jnp.transpose(a, (1, 2, 0, 3)) for a in (star, flux_l, flux_n)), kst, jnp.transpose(fm, (1, 0, 2)), jnp.transpose(fp, (0, 2, 1, 3)), neigh, nface, clus.reshape(1, E), send_l, dmg, count.reshape(1, 1), ymask, coh.reshape(1, E), to_p, from_p)
    hbm = pl.BlockSpec(memory_space=pltpu.HBM)
    vmem = pl.BlockSpec(memory_space=pltpu.VMEM)
    return pl.pallas_call(
        functools.partial(kernel, n),
        out_shape=jax.ShapeDtypeStruct((NQ, NBAS, E), F32),
        in_specs=[hbm] * 12 + [vmem] + [hbm] * 4,
        out_specs=vmem,
        scratch_shapes=[
            pltpu.VMEM((NQ, NBAS, E), F32),
            pltpu.VMEM((NQ, NQ, 3, E), BF16),
            pltpu.VMEM((NQ, NQ, 4, E), BF16),
            pltpu.VMEM((NQ, NQ, 4, E), BF16),
            pltpu.VMEM((3, NBAS, NBAS), F32),
            pltpu.VMEM((NBAS, 4, NBAS), F32),
            pltpu.VMEM((4, NBAS, 4, NBAS), F32),
            pltpu.VMEM((4, E), jnp.int32),
            pltpu.VMEM((4, E), jnp.int32),
            pltpu.VMEM((1, E), jnp.int32),
            pltpu.VMEM((1, 4, NB), jnp.int32),
            pltpu.VMEM((1, E), jnp.int32),
            pltpu.VMEM((NBAS, E), jnp.int32),
            pltpu.VMEM((1, E), F32),
            pltpu.VMEM((NBAS, NBAS), F32),
            pltpu.VMEM((NBAS, NBAS), F32),
            pltpu.SemaphoreType.DMA((17,)),
            pltpu.VMEM((3 * GROUP, 256), BF16),
            pltpu.VMEM((7 * GROUP, 256), BF16),
            pltpu.VMEM((4, 4 * GROUP, 256), BF16),
            pltpu.VMEM((2, GROUP, 256), BF16),
            pltpu.VMEM((NQ, NQ, 3, E), F32),
            pltpu.VMEM((NQ, NQ, 4, E), F32),
            pltpu.VMEM((NQ, NQ, 4, E), F32),
            pltpu.VMEM((4, 2 * E, E), BF16),
            pltpu.VMEM((E, E), BF16),
            pltpu.VMEM((ROWS, E), F32),
            pltpu.VMEM((ROWS, E), F32),
            pltpu.VMEM((ROWS, E), F32),
            pltpu.VMEM((ROWS, E), F32),
            pltpu.VMEM((ROWS, E), F32),
            pltpu.VMEM((ROWS, E), F32),
            *([pltpu.VMEM((7 * GROUP, E), F32)] * 3),
            *([pltpu.VMEM((ROWS, E), F32)] * 4),
            pltpu.VMEM((2 * ROWS, 2 * E), BF16),
            pltpu.VMEM((4, 2 * ROWS, E), BF16),
            pltpu.VMEM((ROWS, E), F32),
            pltpu.VMEM((2, 4, PAIRS, PAD, 128), F32),
            pltpu.VMEM((2, 4, 16, 128), F32),
            pltpu.VMEM((2, 4, PAIRS, PAD, 128), F32),
            pltpu.VMEM((2, 4, 16, 128), F32),
            pltpu.SemaphoreType.DMA((2, 4, 2)),
            pltpu.SemaphoreType.DMA((2, 4, 2)),
        ],
        compiler_params=pltpu.CompilerParams(
            collective_id=0, has_side_effects=True, vmem_limit_bytes=48 << 20
        ),
        name="ader_cycle",
    )(*(a if a.size == 1 else pltpu.with_memory_space_constraint(a, pltpu.HBM) for a in operands))


def solution(mesh):
    n = mesh.shape["dom"]
    return jax.shard_map(
        functools.partial(per_device, n),
        mesh=mesh,
        in_specs=(
            P(None, None, "dom"),
            P(None, None, None, "dom"),
            P(None, None, None, "dom"),
            P(None, None, None, "dom"),
            P(),
            P(),
            P(),
            P(None, "dom"),
            P(None, "dom"),
            P("dom"),
            P("dom", None, None),
            P("dom", None),
            P("dom"),
            P(None, "dom"),
            P("dom"),
            P(),
            P(),
        ),
        out_specs=P(None, None, "dom"),
        check_vma=False,
    )
```

```python
import functools

import jax
import jax.numpy as jnp
from jax import lax
from jax.experimental import pallas as pl
from jax.experimental.pallas import tpu as pltpu
from jax.sharding import PartitionSpec as P

F32, BF16 = jnp.float32, jnp.bfloat16
MESH = pl.DeviceIdType.MESH
OFFSETS = (1, -1, 2, -2)
NQ, NBAS, PAD = 9, 20, 24
ROWS = NQ * PAD
GROUP = 3 * PAD
E, NB = 256, 64
TOP = 112
FRICTION, RELAXATION = 0.6, 0.5


def iota(shape, dim):
    return lax.broadcasted_iota(jnp.int32, shape, dim)


def halves(x):
    hi = x.astype(BF16).astype(F32)
    return hi, x - hi


def right_side(hi, lo):
    rest = jnp.zeros((256 - 3 * GROUP, E), F32)
    return jnp.concatenate([hi, lo, hi, rest], axis=0).astype(BF16)


def dot(a, b):
    return jnp.dot(a, b, preferred_element_type=F32)


def pad_rows(m):
    return jnp.concatenate([m, jnp.zeros((PAD - NBAS, m.shape[1]), F32)], axis=0)


def left_side(mats):
    stacked = jnp.concatenate([pad_rows(m) for m in mats], axis=0)
    hi, lo = halves(stacked)
    lane, row = iota((NBAS, 256), 1), iota((NBAS, 256), 0)
    here = lax.rem(lane, PAD) == row
    one, zero = jnp.ones((NBAS, 256), F32), jnp.zeros((NBAS, 256), F32)
    to_hi = jnp.where(here & (lane < 2 * GROUP), one, zero).astype(BF16)
    to_lo = jnp.where(here & (lane >= 2 * GROUP) & (lane < 3 * GROUP), one, zero).astype(BF16)
    spread = dot(hi.astype(BF16), to_hi) + dot(lo.astype(BF16), to_lo)
    owner = lax.rem(lax.div(iota(spread.shape, 1), PAD), 3)
    blocks = [jnp.where(owner == q, spread, jnp.zeros_like(spread)) for q in range(3)]
    return jnp.concatenate(blocks, axis=0).astype(BF16)


def transposed(m):
    hi, lo = halves(m)
    eye = (iota((NBAS, NBAS), 0) == iota((NBAS, NBAS), 1)).astype(F32).astype(BF16)
    dims = (((1,), (1,)), ((), ()))
    return lax.dot_general(eye, hi.astype(BF16), dims, preferred_element_type=F32) + lax.dot_general(
        eye, lo.astype(BF16), dims, preferred_element_type=F32
    )


def kernel(
    n, h_dof, h_star, h_flux_l, h_flux_n, h_kst, h_minus, h_plus, h_neigh, h_nface, h_clus, h_send, h_dmg, h_count, h_ymask, h_coh,
    h_to, h_from, out,
    dof, star, flux_l, flux_n, kst, f_minus, f_plus, neigh, nface, clus, send_l, dmg, ymask, coh, to_p, from_p, isem,
    bd_d, bd_o, bd_f, bd_p, coef_s, coef_l, coef_n, onehot, onehot_s, x, x1, st, buf, c1, part, y, z, ext, near, ghost, send, recv, ssem, rsem,
):
    me = lax.axis_index("dom")
    pairs = (
        (h_dof, dof), (h_kst, kst), (h_star, star), (h_send, send_l), (h_plus, f_plus), (h_minus, f_minus), (h_flux_l, flux_l),
        (h_flux_n, flux_n), (h_neigh, neigh), (h_nface, nface), (h_clus, clus), (h_to, to_p), (h_from, from_p),
        (h_dmg, dmg), (h_ymask, ymask), (h_coh, coh),
    )
    loads = [pltpu.make_async_copy(src, ref, isem.at[i]) for i, (src, ref) in enumerate(pairs)]
    for load in loads:
        load.start()

    def arrived(*refs):
        for ref in refs:
            for (_, held), load in zip(pairs, loads):
                if held is ref:
                    load.wait()

    def inside(device):
        return (device >= 0) & (device < n)

    barrier = pltpu.get_barrier_semaphore()
    for o in OFFSETS:

        @pl.when(inside(me + o))
        def _():
            pl.semaphore_signal(barrier, inc=1, device_id=(me + o,), device_id_type=MESH)

    partners = sum(jnp.where(inside(me + o), 1, 0) for o in OFFSETS)
    for j, o in enumerate(OFFSETS):

        @pl.when(jnp.logical_not(inside(me - o)))
        def _():
            for turn in range(2):
                recv[turn, j] = jnp.zeros((TOP, 128), F32)

    arrived(dof, kst, star)
    for q in range(NQ):
        x[PAD * q : PAD * (q + 1), :] = pad_rows(dof[q])

    def widen(q, _):
        coef_s[q] = star[q].astype(F32)
        return 0

    lax.fori_loop(0, NQ, widen, 0)
    bd_d[...] = left_side([kst[d] for d in range(3)])
    arrived(send_l)
    for j in range(4):
        listed = send_l[0, j : j + 1, :]
        if j % 2 == 0:
            first = listed
        else:
            both = jnp.concatenate([first, listed], axis=1)
            lanes = slice(128 * (j // 2), 128 * (j // 2) + 128)
            onehot_s[:, lanes] = (iota((E, 128), 0) == both).astype(F32).astype(BF16)

    def tiles():
        return [slice(0, 128), slice(128, 256)]

    def spread(src, lhs, dst, g):
        rows = lhs.shape[0]
        dst[rows * g : rows * (g + 1), :] = dot(lhs[...], right_side(*halves(src[GROUP * g : GROUP * (g + 1), :])))

    def accumulate(y_ref, row_of, coefs, quantities, lanes, accs):
        accs = list(accs)
        for q in quantities:
            for k, (coef, i) in enumerate(coefs):
                yv = y_ref[row_of(q, k) : row_of(q, k) + PAD, lanes]
                for p in range(NQ):
                    term = yv * coef[q, p, i : i + 1, lanes]
                    accs[p] = term if accs[p] is None else accs[p] + term
        return accs

    def held(ref, lanes):
        return [ref[PAD * p : PAD * (p + 1), lanes] for p in range(NQ)]

    def hold(ref, lanes, accs):
        for p in range(NQ):
            ref[PAD * p : PAD * (p + 1), lanes] = accs[p]

    def grouped(src, lhs, coefs, finish):
        nk = len(coefs)
        spread(src, lhs, y, 0)
        for g in range(3):
            if g < 2:
                spread(src, lhs, y, g + 1)
            for lanes in tiles():
                accs = [None] * NQ if g == 0 else held(part, lanes)
                accs = accumulate(y, lambda q, k: (q * nk + k) * PAD, coefs, range(3 * g, 3 * g + 3), lanes, accs)
                if g < 2:
                    hold(part, lanes, accs)
                else:
                    finish(lanes, accs)

    star_coefs = [(coef_s, d) for d in range(3)]
    own_coefs = star_coefs + [(coef_l, f) for f in range(4)]

    def predictor(src, w1, w2):
        grouped(src, bd_d, star_coefs, functools.partial(hold, x1))

        def finish(lanes, accs):
            for p in range(NQ):
                rows = slice(PAD * p, PAD * (p + 1))
                buf[rows, lanes] = src[rows, lanes] + w1(lanes) * x1[rows, lanes] + w2(lanes) * accs[p]

        grouped(x1, bd_d, star_coefs, finish)

    def split_field(field):
        pieces = []
        for g in range(3):
            pieces += list(halves(field[GROUP * g : GROUP * (g + 1), :]))
        return jnp.concatenate(pieces, axis=0).astype(BF16)

    def exchange(turn, j):
        return pltpu.make_async_remote_copy(
            src_ref=send.at[turn, j],
            dst_ref=recv.at[turn, j],
            send_sem=ssem.at[turn, j],
            recv_sem=rsem.at[turn, j],
            device_id=(me + OFFSETS[j],),
            device_id_type=MESH,
        )

    def each(act, turn, sign):
        for j in (2, 0, 3, 1):
            o = OFFSETS[j]

            @pl.when(inside(me + sign * o))
            def _():
                act(exchange(turn, j))

    low = iota((TOP, 128), 1) < NB

    def start_exchange(turn):
        ext[:, 0:E] = split_field(buf)
        picked = dot(ext[:, 0:E], onehot_s[...])
        packed = jnp.concatenate(
            [picked[2 * GROUP * g : 2 * GROUP * g + GROUP] + picked[2 * GROUP * g + GROUP : 2 * GROUP * (g + 1)] for g in range(3)],
            axis=0,
        )
        for t in range(2):
            upper = packed[0:TOP, 128 * t : 128 * t + 128]
            lower = packed[ROWS - TOP : ROWS, 128 * t : 128 * t + 128]
            send[turn, 2 * t] = jnp.where(low, upper, pltpu.roll(lower, NB, 1))
            send[turn, 2 * t + 1] = jnp.where(low, pltpu.roll(upper, NB, 1), lower)
        each(lambda copy: copy.start(), turn, 1)

    def end_exchange(turn):
        each(lambda copy: copy.wait_recv(), turn, -1)
        for t in range(2):
            one, two = recv[turn, 2 * t], recv[turn, 2 * t + 1]
            lanes = slice(128 * t, 128 * t + 128)
            ghost[0:TOP, lanes] = jnp.where(low, one, pltpu.roll(two, NB, 1))
            ghost[ROWS - TOP : ROWS, lanes] = jnp.where(low, pltpu.roll(one, NB, 1), two)
        ext[:, E : 2 * E] = split_field(ghost)

    def own_side(finish):
        grouped(buf, bd_o, own_coefs, finish)

    def near_picks():
        for f in range(4):
            near[f] = dot(ext[:, 0:E], onehot[f, 0:E, :]).astype(BF16)

    def face(f):
        here = [nface[f : f + 1, :] == h for h in range(3)]
        picked = dot(ext[...], onehot[f])
        for g in range(3):
            hi = picked[2 * GROUP * g : 2 * GROUP * g + GROUP]
            lo = picked[2 * GROUP * g + GROUP : 2 * GROUP * (g + 1)]
            four = dot(bd_f[f], right_side(hi, lo))
            for i in range(3):
                part_h = [four[PAD * (4 * i + h) : PAD * (4 * i + h + 1)] for h in range(4)]
                row = f * ROWS + (3 * g + i) * PAD
                z[row : row + PAD, :] = jnp.where(
                    here[0], part_h[0], jnp.where(here[1], part_h[1], jnp.where(here[2], part_h[2], part_h[3]))
                )

    def far_side(finish):
        face(0)
        for f in range(4):
            if f < 3:
                face(f + 1)
            for lanes in tiles():
                accs = accumulate(z, lambda q, k: f * ROWS + q * PAD, [(coef_n, f)], range(NQ), lanes, held(c1, lanes))
                if f < 3:
                    hold(c1, lanes, accs)
                else:
                    finish(lanes, accs)

    predictor(x, lambda lanes: 0.5, lambda lanes: 1.0 / 6.0)
    pl.semaphore_wait(barrier, partners)
    start_exchange(0)
    arrived(f_plus, f_minus, flux_l, flux_n, neigh, nface, clus, to_p, from_p)

    def widen_flux(q, _):
        coef_l[q] = flux_l[q].astype(F32)
        coef_n[q] = flux_n[q].astype(F32)
        return 0

    lax.fori_loop(0, NQ, widen_flux, 0)
    bd_o[...] = left_side([transposed(kst[d]) for d in range(3)] + [-f_minus[:, f, :] for f in range(4)])
    for f in range(4):
        bd_f[f] = left_side([-f_plus[f, :, h, :] for h in range(4)])
    bd_p[0] = left_side([to_p[...]])
    bd_p[1] = left_side([from_p[...]])
    for f in range(4):
        wanted = neigh[f : f + 1, :]
        onehot[f, 0:E, :] = (iota((E, E), 0) == wanted).astype(F32).astype(BF16)
        for j in range(4):
            rows = slice(E + NB * j, E + NB * (j + 1))
            onehot[f, rows, :] = ((iota((NB, E), 0) + E + NB * j) == wanted).astype(F32).astype(BF16)

    own_side(functools.partial(hold, c1))
    end_exchange(0)

    def finish_one(lanes, accs):
        fine = clus[0:1, lanes] == 0
        for p in range(NQ):
            rows = slice(PAD * p, PAD * (p + 1))
            start = x[rows, lanes]
            total = start + accs[p]
            c1[rows, lanes] = total
            st[rows, lanes] = jnp.where(fine, total, start)

    far_side(finish_one)

    def weight(fine_one, coarse_one):
        return lambda lanes: jnp.where(clus[0:1, lanes] == 0, F32(fine_one), F32(coarse_one))

    predictor(st, weight(0.5, 1.5), weight(1.0 / 6.0, 7.0 / 6.0))
    start_exchange(1)

    def finish_two(lanes, accs):
        for p in range(NQ):
            rows = slice(PAD * p, PAD * (p + 1))
            c1[rows, lanes] = c1[rows, lanes] + accs[p]

    own_side(finish_two)
    arrived(dmg, ymask, coh)
    listed = (iota((E, E), 0) == dmg[...]) & (iota((E, E), 1) < h_count[...])
    live = lax.dot_general(
        jnp.ones((8, E), BF16), listed.astype(F32).astype(BF16), (((1,), (1,)), ((), ())), preferred_element_type=F32
    )[0:1]
    end_exchange(1)
    far_side(functools.partial(hold, c1))

    points = []
    for g in range(2):
        got = dot(bd_p[0], right_side(*halves(c1[GROUP * g : GROUP * (g + 1), :])))
        points += [got[PAD * i : PAD * (i + 1)] for i in range(3)]
    pressure = (points[0] + points[1] + points[2]) / 3.0
    dev = [points[i] - pressure for i in range(3)] + points[3:]
    tau = jnp.sqrt(
        0.5 * (dev[0] * dev[0] + dev[1] * dev[1] + dev[2] * dev[2])
        + (dev[3] * dev[3] + dev[4] * dev[4] + dev[5] * dev[5])
    )
    strength = coh[0:1, :]
    limit = jnp.maximum(strength - FRICTION * pressure, 0.5 * strength)
    rate = RELAXATION * (limit / jnp.maximum(tau, limit) - 1.0)
    marked = jnp.concatenate([ymask[...], jnp.zeros((PAD - NBAS, E), jnp.int32)], axis=0)
    rate = jnp.where((marked == 1) & (live > 0.5), rate, jnp.zeros_like(rate))
    for g in range(2):
        change = jnp.concatenate([rate * dev[3 * g + i] for i in range(3)], axis=0)
        got = dot(bd_p[1], right_side(*halves(change)))
        for i in range(3):
            q = 3 * g + i
            out[q] = c1[PAD * q : PAD * q + NBAS, :] + got[PAD * i : PAD * i + NBAS]
    for q in range(6, NQ):
        out[q] = c1[PAD * q : PAD * q + NBAS, :]
    for turn in range(2):
        each(lambda copy: copy.wait_send(), turn, 1)


def per_device(n, dof, star, flux_l, flux_n, kst, fm, fp, neigh, nface, clus, send_l, dmg, count, ymask, coh, to_p, from_p):
    operands = (dof, *(jnp.transpose(a, (1, 2, 0, 3)) for a in (star, flux_l, flux_n)), kst, jnp.transpose(fm, (1, 0, 2)), jnp.transpose(fp, (0, 2, 1, 3)), neigh, nface, clus.reshape(1, E), send_l, dmg, count.reshape(1, 1), ymask, coh.reshape(1, E), to_p, from_p)
    hbm = pl.BlockSpec(memory_space=pltpu.HBM)
    vmem = pl.BlockSpec(memory_space=pltpu.VMEM)
    return pl.pallas_call(
        functools.partial(kernel, n),
        out_shape=jax.ShapeDtypeStruct((NQ, NBAS, E), F32),
        in_specs=[hbm] * 12 + [vmem] + [hbm] * 4,
        out_specs=vmem,
        scratch_shapes=[
            pltpu.VMEM((NQ, NBAS, E), F32),
            pltpu.VMEM((NQ, NQ, 3, E), BF16),
            pltpu.VMEM((NQ, NQ, 4, E), BF16),
            pltpu.VMEM((NQ, NQ, 4, E), BF16),
            pltpu.VMEM((3, NBAS, NBAS), F32),
            pltpu.VMEM((NBAS, 4, NBAS), F32),
            pltpu.VMEM((4, NBAS, 4, NBAS), F32),
            pltpu.VMEM((4, E), jnp.int32),
            pltpu.VMEM((4, E), jnp.int32),
            pltpu.VMEM((1, E), jnp.int32),
            pltpu.VMEM((1, 4, NB), jnp.int32),
            pltpu.VMEM((1, E), jnp.int32),
            pltpu.VMEM((NBAS, E), jnp.int32),
            pltpu.VMEM((1, E), F32),
            pltpu.VMEM((NBAS, NBAS), F32),
            pltpu.VMEM((NBAS, NBAS), F32),
            pltpu.SemaphoreType.DMA((17,)),
            pltpu.VMEM((3 * GROUP, 256), BF16),
            pltpu.VMEM((7 * GROUP, 256), BF16),
            pltpu.VMEM((4, 4 * GROUP, 256), BF16),
            pltpu.VMEM((2, GROUP, 256), BF16),
            pltpu.VMEM((NQ, NQ, 3, E), F32),
            pltpu.VMEM((NQ, NQ, 4, E), F32),
            pltpu.VMEM((NQ, NQ, 4, E), F32),
            pltpu.VMEM((4, 2 * E, E), BF16),
            pltpu.VMEM((E, E), BF16),
            pltpu.VMEM((ROWS, E), F32),
            pltpu.VMEM((ROWS, E), F32),
            pltpu.VMEM((ROWS, E), F32),
            pltpu.VMEM((ROWS, E), F32),
            pltpu.VMEM((ROWS, E), F32),
            pltpu.VMEM((ROWS, E), F32),
            pltpu.VMEM((7 * ROWS, E), F32),
            pltpu.VMEM((4 * ROWS, E), F32),
            pltpu.VMEM((2 * ROWS, 2 * E), BF16),
            pltpu.VMEM((4, 2 * ROWS, E), BF16),
            pltpu.VMEM((ROWS, E), F32),
            pltpu.VMEM((2, 4, TOP, 128), F32),
            pltpu.VMEM((2, 4, TOP, 128), F32),
            pltpu.SemaphoreType.DMA((2, 4)),
            pltpu.SemaphoreType.DMA((2, 4)),
        ],
        compiler_params=pltpu.CompilerParams(
            collective_id=0, has_side_effects=True, vmem_limit_bytes=48 << 20
        ),
        name="ader_cycle",
    )(*(a if a.size == 1 else pltpu.with_memory_space_constraint(a, pltpu.HBM) for a in operands))


def solution(mesh):
    n = mesh.shape["dom"]
    return jax.shard_map(
        functools.partial(per_device, n),
        mesh=mesh,
        in_specs=(
            P(None, None, "dom"),
            P(None, None, None, "dom"),
            P(None, None, None, "dom"),
            P(None, None, None, "dom"),
            P(),
            P(),
            P(),
            P(None, "dom"),
            P(None, "dom"),
            P("dom"),
            P("dom", None, None),
            P("dom", None),
            P("dom"),
            P(None, "dom"),
            P("dom"),
            P(),
            P(),
        ),
        out_specs=P(None, None, "dom"),
        check_vma=False,
    )
```
